128 devices in a mesh: dp: 64 (over z, y, x_hi, core), feat: 2 (over x_lo).
Axes of the slice: x: 4 (x_hi: 2, x_lo: 2; x = x_hi * 2 + x_lo), y: 4, z: 4, core: 2. Of those that a mesh axis runs over, the one named last changes fastest.
Arguments:
- embeddings: bfloat16 [131072, 1024], P('dp', 'feat')
- assignments: int32 [131072], P('dp'), may hold values from 0 to 511, as said below
- order_index: int32 [131072], P('dp'), may hold values from 0 to 131071, each once
- cluster_blocks: int32 [512], replicated, may hold values from 1 to 4, as said below
Outputs:
- centroids: bfloat16 [512, 1024], P('dp', 'feat')
- centroid_sim: float32 [131072], P('dp')
- earlier_max: float32 [131072], P('dp')
The draws below stay inside these ranges and needn't reach their ends.
Inputs may be any that keep to these rules, and one draw needn't show every extreme that they name: `assignments`: every cluster holds at least one row. The rows of one index of dp name one cluster at most 8 times, and on every index some cluster exactly 8 times. `cluster_blocks`: the number of rows of the cluster divided by 128, rounded up; some cluster has 512 rows.
All inputs are finite; a program needn't handle non-finite values.
Results may differ from the reference program's by a relative error of at most 0.0012.
Values may be sent and summed in bfloat16 or wider, within the bound.
A program may use at most 64 MiB of HBM per device.

```python
from functools import partial
import jax
import jax.numpy as jnp
from jax import lax

D = 1024
ROWS_DEV = 2048
BLOCK = 128
K = 512
ROWS = 131072
MOST = 8
CAPACITY = 512


def cluster_plan(key):
    devices = ROWS // ROWS_DEV
    slots = K * MOST
    hottest = max(1, K // 64)
    base_key = jax.random.fold_in(key, 101)
    key_weight, key_raw, key_hot, key_shuffle = jax.random.split(base_key, 4)
    weights = jax.random.randint(key_weight, (K,), 1, 9)
    raw = jax.random.randint(key_raw, (devices, K, MOST), 0, 8192) * weights[None, :, None]
    hot_order = jax.random.permutation(key_hot, K)
    is_hot = jnp.zeros((K,), jnp.int32).at[hot_order[:hottest]].set(1)
    device_ids = jnp.arange(devices)[:, None, None]
    cluster_ids = jnp.arange(K)[None, :, None]
    slot_ids = jnp.arange(MOST)[None, None, :]
    covers = (cluster_ids % devices == device_ids) & (slot_ids == 0)
    score = jnp.where(is_hot[None, :, None] == 1, 65538, jnp.where(covers, 65537, raw))
    distinct = score * slots + (cluster_ids * MOST + slot_ids)
    top_values, picked = lax.top_k(distinct.reshape(devices, slots), ROWS_DEV)
    chosen = (picked // MOST).astype(jnp.int32)
    chosen = jax.random.permutation(key_shuffle, chosen, axis=1, independent=True)
    return chosen.reshape(ROWS).astype(jnp.int32)


def draw_assignments(key, part):
    return cluster_plan(key)


def draw_cluster_blocks(key, part):
    clusters = cluster_plan(key)
    sizes = jax.ops.segment_sum(jnp.ones((ROWS,), jnp.int32), clusters, num_segments=K)
    return ((sizes + 127) // 128).astype(jnp.int32)


def draw_embeddings(key, part):
    clusters = cluster_plan(key)
    centre_key = jax.random.fold_in(key, 201)
    noise_key = jax.random.fold_in(key, 202)
    centres = jax.random.normal(centre_key, (K, D), jnp.float32)
    noise = jax.random.normal(noise_key, (ROWS, D), jnp.float32)
    values = 0.8 * centres[clusters] + noise
    return values.astype(jnp.bfloat16)


def setup_inputs(seed: int = 0) -> dict:
    splits = jax.random.split(jax.random.key(seed), 5)
    return {
        "embeddings": draw_embeddings(jax.random.fold_in(splits[4], 71), 0),
        "assignments": draw_assignments(jax.random.fold_in(splits[4], 71), 0),
        "order_index": jax.random.permutation(splits[2], ROWS).astype(jnp.int32),
        "cluster_blocks": draw_cluster_blocks(jax.random.fold_in(splits[4], 71), 0),
    }


epsilon = 1e-06

def masked_best(unit_rows, row_order, used_rows):
    leading = unit_rows[:used_rows]
    key_order = row_order[:used_rows]
    similar = jnp.dot(leading, leading.T, precision=lax.Precision.HIGHEST, preferred_element_type=jnp.float32)
    earlier = (key_order[None, :] < key_order[:, None]) & (key_order[None, :] >= 0)
    best_match = lax.optimization_barrier(jnp.max(jnp.where(earlier, similar, jnp.float32(-1.0)), axis=1))
    filler = jnp.full((unit_rows.shape[0] - used_rows,), -1.0, jnp.float32)
    return jnp.concatenate([best_match, filler])

def reference(embeddings, assignments, order_index, cluster_blocks):
    values = embeddings.astype(jnp.float32)
    counts_int = jax.ops.segment_sum(jnp.ones((ROWS,), jnp.int32), assignments, num_segments=K)
    counts = counts_int.astype(jnp.float32)
    sums = jax.ops.segment_sum(values, assignments, num_segments=K)
    averages = sums / counts[:, None]
    centre_norms = lax.optimization_barrier(jnp.sum(averages * averages, axis=1))
    centroids = (averages / jnp.sqrt(centre_norms + epsilon)[:, None]).astype(jnp.bfloat16)
    squares = lax.optimization_barrier(jnp.sum(values * values, axis=1))
    products = lax.optimization_barrier(jnp.sum(values * centroids[assignments].astype(jnp.float32), axis=1))
    lengths = jnp.sqrt(squares + epsilon)
    centroid_sim = products / lengths
    unit_rows = (values / lengths[:, None]).astype(jnp.bfloat16)
    sort_order = jnp.argsort(assignments, stable=True).astype(jnp.int32)
    sorted_rows = unit_rows[sort_order].astype(jnp.float32)
    sorted_order = order_index[sort_order]
    sorted_cluster = assignments[sort_order]
    first_slot = (jnp.cumsum(counts_int) - counts_int).astype(jnp.int32)
    padded_rows = jnp.concatenate([sorted_rows, jnp.zeros((CAPACITY, D), jnp.float32)])
    padded_order = jnp.concatenate([sorted_order, jnp.full((CAPACITY,), -1, jnp.int32)])
    branches = [partial(masked_best, used_rows=(level + 1) * BLOCK) for level in range(CAPACITY // BLOCK)]

    def one_cluster(cluster):
        begin = first_slot[cluster]
        rows_here = lax.dynamic_slice_in_dim(padded_rows, begin, CAPACITY, 0)
        order_here = lax.dynamic_slice_in_dim(padded_order, begin, CAPACITY, 0)
        order_here = jnp.where(jnp.arange(CAPACITY, dtype=jnp.int32) < counts_int[cluster], order_here, -1)
        return lax.switch(cluster_blocks[cluster] - 1, branches, rows_here, order_here)
    results = lax.map(one_cluster, jnp.arange(K, dtype=jnp.int32))
    within = jnp.arange(ROWS, dtype=jnp.int32) - first_slot[sorted_cluster]
    sorted_best = results.reshape(-1)[sorted_cluster * CAPACITY + within]
    earlier_max = jnp.zeros((ROWS,), jnp.float32).at[sort_order].set(sorted_best)
    return (centroids, centroid_sim, earlier_max)
```

```python
from functools import partial

import jax
import jax.numpy as jnp
from jax import lax
from jax.experimental import pallas as pl
from jax.experimental.pallas import tpu as pltpu
from jax.sharding import PartitionSpec as P

epsilon = 1e-06
MESH = pl.DeviceIdType.MESH
NT = (((1,), (1,)), ((), ()))
TN = (((0,), (0,)), ((), ()))

LOCAL = 4
SLOTS = 8
SOURCES = 64
DEVICES = 128
CHUNK = 32
BIG = float(2**20)


def iota(shape, axis):
    return lax.broadcasted_iota(jnp.int32, shape, axis)


def position():
    dp = lax.axis_index("dp")
    feat = lax.axis_index("feat")
    return dp, feat, (dp // 16, (dp // 4) % 4, (dp // 2) % 2 * 2 + feat, dp % 2)


def shifted(place, k):
    z, y, x, core = place
    tz = (z + k % 4) % 4
    ty = (y + (k // 4) % 4) % 4
    tx = (x + (k // 16) % 4) % 4
    tc = (core + k // 64) % 2
    return ((tz * 4 + ty) * 2 + tx // 2) * 2 + tc, tx % 2


def shifted_owner(place, k):
    z, y, x, core = place
    tz = (z + (k & 3)) & 3
    ty = (y + ((k >> 2) & 3)) & 3
    tx = (x + ((k >> 4) & 3)) & 3
    tc = (core + (k >> 6)) & 1
    return (tz << 5) + (ty << 3) + ((tx >> 1) << 2) + (tc << 1) + (tx & 1)


def onehot(condition):
    return jnp.where(condition, 1.0, 0.0).astype(jnp.bfloat16)


def thirds(values):
    high = values.astype(jnp.bfloat16)
    rest = values - high.astype(jnp.float32)
    middle = rest.astype(jnp.bfloat16)
    low = (rest - middle.astype(jnp.float32)).astype(jnp.bfloat16)
    return high, middle, low


def f32_dot(a, b, dims):
    return lax.dot_general(a, b, dims, preferred_element_type=jnp.float32)


def kernel(
    rows_hbm,
    assign_ref,
    order_ref,
    cent_ref,
    sim_ref,
    best_ref,
    rows,
    slot_of_row,
    hits_owner,
    send,
    recv,
    meta_send,
    meta_recv,
    key_cols,
    key_rows,
    cent_mine,
    cent_other,
    back_send,
    back_recv,
    load_sem,
    send_sem,
    recv_sem,
    meta_send_sem,
    meta_recv_sem,
    cent_send_sem,
    cent_recv_sem,
    back_send_sem,
    back_recv_sem,
):
    dp, feat, place = position()
    n_rows = rows.shape[0]
    width = rows.shape[1]
    members = SOURCES * SLOTS
    load = pltpu.make_async_copy(rows_hbm, rows, load_sem)
    load.start()

    barrier = pltpu.get_barrier_semaphore()

    def greet(k, carry):
        tdp, tfeat = shifted(place, k)
        pl.semaphore_signal(barrier, inc=1, device_id=(tdp, tfeat), device_id_type=MESH)
        return carry

    lax.fori_loop(1, DEVICES, greet, 0)

    part = 256
    n_clusters = DEVICES * LOCAL
    before = onehot(iota((part, part), 0) < iota((part, part), 1))
    ones = jnp.ones((part, part), jnp.bfloat16)

    counted = jnp.zeros((n_clusters, part), jnp.float32)
    for block in range(n_rows // part):
        piece = assign_ref[:, block * part : (block + 1) * part]
        member = iota((n_clusters, part), 0) == piece
        member_b = onehot(member)
        ahead = jnp.dot(member_b, before, preferred_element_type=jnp.float32) + counted
        rank = jnp.sum(jnp.where(member, ahead, 0.0), axis=0, keepdims=True)
        slot_of_row[:, block * part : (block + 1) * part] = piece * SLOTS + rank.astype(jnp.int32)
        if block + 1 < n_rows // part:
            counted = counted + jnp.dot(member_b, ones, preferred_element_type=jnp.float32)

    slots = slot_of_row[...]
    own_slots = LOCAL * SLOTS
    hits_owner[...] = onehot(iota((DEVICES, n_rows), 0) == (slots >> 5))
    orders = order_ref[...]
    line = iota((DEVICES, n_rows), 0)
    kind = line >> 5
    digit = jnp.where(
        kind == 0,
        orders >> 14,
        jnp.where(kind == 1, (orders >> 7) & 127, jnp.where(kind == 2, orders & 127, 1)),
    )
    digits = jnp.where((line & 31) == (slots & 31), digit, 0).astype(jnp.float32)
    meta = f32_dot(hits_owner[...], digits.astype(jnp.bfloat16), NT)
    meta_send[:, 0, :] = meta

    load.wait()
    pl.semaphore_wait(barrier, DEVICES - 1)

    def meta_out(k, carry):
        tdp, tfeat = shifted(place, k)

        @pl.when(tfeat == feat)
        def _():
            pltpu.make_async_remote_copy(
                meta_send.at[tdp * 2 + feat],
                meta_recv.at[dp],
                meta_send_sem,
                meta_recv_sem,
                device_id=(tdp, feat),
                device_id_type=MESH,
            ).start()

        return carry

    lax.fori_loop(1, DEVICES, meta_out, 0)
    pltpu.make_async_copy(meta_send.at[dp * 2 + feat], meta_recv.at[dp], meta_recv_sem).start()

    n_chunks = DEVICES // CHUNK

    def pack(step, carry):
        local = step // n_chunks
        chunk = step % n_chunks
        q = iota((CHUNK * SLOTS, 1), 0)
        owner = shifted_owner(place, chunk * CHUNK + (q >> 3))
        wanted = owner * own_slots + local * SLOTS + (q & 7)
        hits = onehot(wanted == slot_of_row[...])
        packed = jnp.dot(hits, rows[...], preferred_element_type=jnp.float32)
        send[local, pl.ds(chunk * CHUNK, CHUNK)] = packed.reshape(CHUNK, SLOTS, width).astype(
            jnp.bfloat16
        )

        def ship(i, carry):
            k = chunk * CHUNK + i
            tdp, tfeat = shifted(place, k)
            pltpu.make_async_remote_copy(
                send.at[local, k],
                recv.at[local, feat, dp],
                send_sem.at[local],
                recv_sem.at[local],
                device_id=(tdp, tfeat),
                device_id_type=MESH,
            ).start()
            return carry

        @pl.when(chunk == 0)
        def _():
            pltpu.make_async_copy(
                send.at[local, 0], recv.at[local, feat, dp], recv_sem.at[local]
            ).start()
            lax.fori_loop(1, CHUNK, ship, 0)

        @pl.when(chunk > 0)
        def _():
            lax.fori_loop(0, CHUNK, ship, 0)

        return carry

    lax.fori_loop(0, LOCAL * n_chunks, pack, 0)

    pltpu.make_async_copy(meta_recv, meta_recv, meta_recv_sem).wait()
    meta_in = meta_recv[:, 0, :].astype(jnp.bfloat16)
    of_source = onehot(iota((SOURCES, members), 0) == (iota((SOURCES, members), 1) >> 3))

    def scale_of(index):
        kind = index >> 5
        return jnp.where(
            kind == 0, 16384.0, jnp.where(kind == 1, 128.0, jnp.where(kind == 2, 1.0, -BIG))
        )

    across = f32_dot(meta_in, of_source, TN) * scale_of(iota((DEVICES, members), 0))
    down = f32_dot(of_source, meta_in, TN) * scale_of(iota((members, DEVICES), 1))
    filled_counts = []
    for local in range(LOCAL):
        pick = (iota((DEVICES, members), 0) & 31) == local * SLOTS + (iota((DEVICES, members), 1) & 7)
        key_rows[local] = BIG + jnp.sum(jnp.where(pick, across, 0.0), axis=0, keepdims=True)
        pick = (iota((members, DEVICES), 1) & 31) == local * SLOTS + (iota((members, DEVICES), 0) & 7)
        key_cols[local] = BIG + jnp.sum(jnp.where(pick, down, 0.0), axis=1, keepdims=True)

    lane = iota((members, DEVICES), 1)
    slot_of_member = iota((members, DEVICES), 0) & 7
    back = jnp.zeros((SOURCES, DEVICES), jnp.float32)
    for local in range(LOCAL):
        pltpu.make_async_copy(recv.at[local], recv.at[local], recv_sem.at[local]).wait()
        values = jnp.concatenate(
            [recv[local, h].astype(jnp.float32).reshape(members, width) for h in range(2)], axis=1
        )
        order_row = key_rows[local]
        order_col = key_cols[local]
        count = jnp.sum(jnp.where(order_row < BIG, 1.0, 0.0), axis=1, keepdims=True)
        squares = jnp.sum(values * values, axis=1, keepdims=True)
        lengths = jnp.sqrt(squares + epsilon)
        averages = jnp.sum(values, axis=0, keepdims=True) / count
        norm = jnp.sum(averages * averages, axis=1, keepdims=True)
        centroid = (averages / jnp.sqrt(norm + epsilon)).astype(jnp.bfloat16).astype(jnp.float32)
        for h in range(2):
            half = centroid[:, h * width : (h + 1) * width]
            cent_mine[h, local : local + 1] = half
            cent_mine[h, local + LOCAL : local + LOCAL + 1] = half
        products = jnp.sum(values * centroid, axis=1, keepdims=True)
        inverse = 1.0 / lengths
        sim = products * inverse
        unit = (values * inverse).astype(jnp.bfloat16)
        similar = f32_dot(unit, unit, NT)
        best = jnp.max(jnp.where(order_col < order_row, similar, -1.0), axis=0, keepdims=True)
        best_of_source = jnp.where(
            iota((SOURCES, members), 0) == (iota((SOURCES, members), 1) >> 3), best, 0.0
        )
        to_lane = onehot(lane == local * SLOTS + slot_of_member)
        sim_lanes = jnp.where(lane == (LOCAL + local) * SLOTS + slot_of_member, sim, 0.0)
        for piece in thirds(best_of_source):
            back = back + jnp.dot(piece, to_lane, preferred_element_type=jnp.float32)
        for piece in thirds(sim_lanes):
            back = back + jnp.dot(of_source, piece, preferred_element_type=jnp.float32)

    back_send[:, 0, :] = back
    swap = pltpu.make_async_remote_copy(
        cent_mine.at[1 - feat],
        cent_other,
        cent_send_sem,
        cent_recv_sem,
        device_id=(dp, 1 - feat),
        device_id_type=MESH,
    )

    def back_out(k, carry):
        tdp, tfeat = shifted(place, k)
        pltpu.make_async_remote_copy(
            back_send.at[tdp],
            back_recv.at[dp * 2 + feat],
            back_send_sem,
            back_recv_sem,
            device_id=(tdp, tfeat),
            device_id_type=MESH,
        ).start()
        return carry

    lax.fori_loop(1, DEVICES, back_out, 0)
    pltpu.make_async_copy(back_send.at[dp], back_recv.at[dp * 2 + feat], back_recv_sem).start()
    swap.start()

    pltpu.make_async_copy(back_recv, back_recv, back_recv_sem).wait()
    table = back_recv[:, 0, :]
    hits = hits_owner[...]
    found = jnp.zeros((DEVICES, n_rows), jnp.float32)
    for piece in thirds(table):
        found = found + f32_dot(piece, hits, TN)
    own_slot = slot_of_row[...] & 31
    line = iota((own_slots, n_rows), 0)
    mine = line == own_slot
    best_ref[...] = jnp.sum(jnp.where(mine, found[:own_slots], 0.0), axis=0, keepdims=True)
    sim_ref[...] = jnp.sum(
        jnp.where(mine, found[own_slots : 2 * own_slots], 0.0), axis=0, keepdims=True
    )
    swap.wait()
    owned_here = (iota((2 * LOCAL, width), 0) // LOCAL) == feat
    cent_ref[...] = jnp.where(owned_here, cent_mine[feat], cent_other[...]).astype(jnp.bfloat16)

    for local in range(LOCAL):
        sent = send.at[local, pl.ds(0, DEVICES - 1)]
        pltpu.make_async_copy(sent, sent, send_sem.at[local]).wait()
    sent = meta_send.at[pl.ds(0, SOURCES - 1)]
    pltpu.make_async_copy(sent, sent, meta_send_sem).wait()
    sent = back_recv.at[pl.ds(0, DEVICES - 1)]
    pltpu.make_async_copy(sent, sent, back_send_sem).wait()


def body(embeddings, assignments, order_index, cluster_blocks):
    n_rows, width = embeddings.shape
    members = SOURCES * SLOTS
    vmem = pl.BlockSpec(memory_space=pltpu.VMEM)
    dma = pltpu.SemaphoreType.DMA
    centroids, sims, bests = pl.pallas_call(
        kernel,
        out_shape=(
            jax.ShapeDtypeStruct((2 * LOCAL, width), jnp.bfloat16),
            jax.ShapeDtypeStruct((1, n_rows), jnp.float32),
            jax.ShapeDtypeStruct((1, n_rows), jnp.float32),
        ),
        in_specs=[pl.BlockSpec(memory_space=pl.ANY), vmem, vmem],
        out_specs=(vmem, vmem, vmem),
        scratch_shapes=[
            pltpu.VMEM((n_rows, width), jnp.bfloat16),
            pltpu.VMEM((1, n_rows), jnp.int32),
            pltpu.VMEM((DEVICES, n_rows), jnp.bfloat16),
            pltpu.VMEM((LOCAL, DEVICES, SLOTS, width), jnp.bfloat16),
            pltpu.VMEM((LOCAL, 2, SOURCES, SLOTS, width), jnp.bfloat16),
            pltpu.VMEM((DEVICES, 1, DEVICES), jnp.float32),
            pltpu.VMEM((SOURCES, 1, DEVICES), jnp.float32),
            pltpu.VMEM((LOCAL, members, 1), jnp.float32),
            pltpu.VMEM((LOCAL, 1, members), jnp.float32),
            pltpu.VMEM((2, 2 * LOCAL, width), jnp.float32),
            pltpu.VMEM((2 * LOCAL, width), jnp.float32),
            pltpu.VMEM((SOURCES, 1, DEVICES), jnp.float32),
            pltpu.VMEM((DEVICES, 1, DEVICES), jnp.float32),
            dma(()),
            dma((LOCAL,)),
            dma((LOCAL,)),
            dma(()),
            dma(()),
            dma(()),
            dma(()),
            dma(()),
            dma(()),
        ],
        compiler_params=pltpu.CompilerParams(
            collective_id=0, has_side_effects=True, vmem_limit_bytes=56 * 2**20
        ),
        name="dedup_window",
    )(embeddings, assignments.reshape(1, n_rows), order_index.reshape(1, n_rows))
    return centroids, sims.reshape(n_rows), bests.reshape(n_rows)


def solution(mesh):
    return jax.shard_map(
        body,
        mesh=mesh,
        in_specs=(P("dp", "feat"), P("dp"), P("dp"), P()),
        out_specs=(P("dp", "feat"), P("dp"), P("dp")),
        check_vma=False,
    )
```

```python
from functools import partial

import jax
import jax.numpy as jnp
from jax import lax
from jax.experimental import pallas as pl
from jax.experimental.pallas import tpu as pltpu
from jax.sharding import PartitionSpec as P

epsilon = 1e-06
MESH = pl.DeviceIdType.MESH
NT = (((1,), (1,)), ((), ()))
TN = (((0,), (0,)), ((), ()))

LOCAL = 4
SLOTS = 8
SOURCES = 64
DEVICES = 128
CHUNK = 32
BIG = float(2**20)


def iota(shape, axis):
    return lax.broadcasted_iota(jnp.int32, shape, axis)


def position():
    dp = lax.axis_index("dp")
    feat = lax.axis_index("feat")
    return dp, feat, (dp // 16, (dp // 4) % 4, (dp // 2) % 2 * 2 + feat, dp % 2)


def each_device(place, visit, groups=(0, 8)):
    z, y, x, core = place
    planes = [(z + d) % 4 * 16 for d in range(4)]
    lines = [(y + d) % 4 * 4 for d in range(4)]
    corners = [planes[i % 4] + lines[i // 4] for i in range(16)]

    def column(group, carry):
        tx = (x + group % 4) % 4
        tc = (core + group // 4) % 2
        inner = tx // 2 * 2 + tc
        for i in range(1 if isinstance(group, int) and group == 0 else 0, 16):
            visit(group * 16 + i, corners[i] + inner, tx % 2)
        return carry

    first, last = groups
    if isinstance(first, int) and first == 0:
        column(0, 0)
        first = 1
    lax.fori_loop(first, last, column, 0)


def shifted_owner(place, k):
    z, y, x, core = place
    tz = (z + (k & 3)) & 3
    ty = (y + ((k >> 2) & 3)) & 3
    tx = (x + ((k >> 4) & 3)) & 3
    tc = (core + (k >> 6)) & 1
    return (tz << 5) + (ty << 3) + ((tx >> 1) << 2) + (tc << 1) + (tx & 1)


def onehot(condition):
    return jnp.where(condition, 1.0, 0.0).astype(jnp.bfloat16)


def thirds(values):
    high = values.astype(jnp.bfloat16)
    rest = values - high.astype(jnp.float32)
    middle = rest.astype(jnp.bfloat16)
    low = (rest - middle.astype(jnp.float32)).astype(jnp.bfloat16)
    return high, middle, low


def f32_dot(a, b, dims):
    return lax.dot_general(a, b, dims, preferred_element_type=jnp.float32)


def kernel(
    rows_hbm,
    assign_ref,
    order_ref,
    cent_ref,
    sim_ref,
    best_ref,
    rows,
    slot_of_row,
    hits_owner,
    send,
    recv,
    meta_send,
    meta_recv,
    key_cols,
    key_rows,
    cent_mine,
    cent_other,
    back_send,
    back_recv,
    load_sem,
    send_sem,
    recv_sem,
    meta_send_sem,
    meta_recv_sem,
    cent_send_sem,
    cent_recv_sem,
    back_send_sem,
    back_recv_sem,
):
    dp, feat, place = position()
    n_rows = rows.shape[0]
    width = rows.shape[1]
    members = SOURCES * SLOTS
    load = pltpu.make_async_copy(rows_hbm, rows, load_sem)
    load.start()

    barrier = pltpu.get_barrier_semaphore()

    def greet(k, tdp, tfeat):
        pl.semaphore_signal(barrier, inc=1, device_id=(tdp, tfeat), device_id_type=MESH)

    each_device(place, greet)

    part = 256
    n_clusters = DEVICES * LOCAL
    before = onehot(iota((part, part), 0) < iota((part, part), 1))
    ones = jnp.ones((part, part), jnp.bfloat16)

    counted = jnp.zeros((n_clusters, part), jnp.float32)
    for block in range(n_rows // part):
        piece = assign_ref[:, block * part : (block + 1) * part]
        member = iota((n_clusters, part), 0) == piece
        member_b = onehot(member)
        ahead = jnp.dot(member_b, before, preferred_element_type=jnp.float32) + counted
        rank = jnp.sum(jnp.where(member, ahead, 0.0), axis=0, keepdims=True)
        slot_of_row[:, block * part : (block + 1) * part] = piece * SLOTS + rank.astype(jnp.int32)
        if block + 1 < n_rows // part:
            counted = counted + jnp.dot(member_b, ones, preferred_element_type=jnp.float32)

    slots = slot_of_row[...]
    own_slots = LOCAL * SLOTS
    hits_owner[...] = onehot(iota((DEVICES, n_rows), 0) == (slots >> 5))
    orders = order_ref[...]
    line = iota((DEVICES, n_rows), 0)
    kind = line >> 5
    digit = jnp.where(
        kind == 0,
        orders >> 14,
        jnp.where(kind == 1, (orders >> 7) & 127, jnp.where(kind == 2, orders & 127, 1)),
    )
    digits = jnp.where((line & 31) == (slots & 31), digit, 0).astype(jnp.float32)
    meta = f32_dot(hits_owner[...], digits.astype(jnp.bfloat16), NT)
    meta_send[:, 0, :] = meta

    def pack(local, chunk):
        q = iota((CHUNK * SLOTS, 1), 0)
        owner = shifted_owner(place, chunk * CHUNK + (q >> 3))
        wanted = owner * own_slots + local * SLOTS + (q & 7)
        hits = onehot(wanted == slot_of_row[...])
        packed = jnp.dot(hits, rows[...], preferred_element_type=jnp.float32)
        send[local, pl.ds(chunk * CHUNK, CHUNK)] = packed.reshape(CHUNK, SLOTS, width).astype(
            jnp.bfloat16
        )

    def ship_to(local):
        def ship(k, tdp, tfeat):
            pltpu.make_async_remote_copy(
                send.at[local, k],
                recv.at[local, feat, dp],
                send_sem.at[local],
                recv_sem.at[local],
                device_id=(tdp, tfeat),
                device_id_type=MESH,
            ).start()

        return ship

    def keep(local):
        pltpu.make_async_copy(
            send.at[local, 0], recv.at[local, feat, dp], recv_sem.at[local]
        ).start()

    n_chunks = DEVICES // CHUNK
    chunk_groups = CHUNK // 16

    def pack_first(chunk, carry):
        pack(0, chunk)
        return carry

    load.wait()
    lax.fori_loop(0, n_chunks, pack_first, 0)
    pl.semaphore_wait(barrier, DEVICES - 1)
    each_device(place, ship_to(0))
    keep(0)

    z, y, x, core = place

    def meta_out(group, carry):
        tz = (z + group // 4) % 4
        ty = (y + group % 4) % 4
        for i in range(4):
            tdp = ((tz * 4 + ty) * 2 + (x // 2 + i // 2) % 2) * 2 + (core + i) % 2

            def start():
                pltpu.make_async_remote_copy(
                    meta_send.at[tdp * 2 + feat],
                    meta_recv.at[dp],
                    meta_send_sem,
                    meta_recv_sem,
                    device_id=(tdp, feat),
                    device_id_type=MESH,
                ).start()

            if i == 0:
                pl.when(group > 0)(start)
            else:
                start()
        return carry

    lax.fori_loop(0, 16, meta_out, 0)
    pltpu.make_async_copy(meta_send.at[dp * 2 + feat], meta_recv.at[dp], meta_recv_sem).start()

    def phase(local, carry):
        pack(local, 0)
        each_device(place, ship_to(local), (0, chunk_groups))
        keep(local)

        def more(chunk, carry):
            pack(local, chunk)
            each_device(place, ship_to(local), (chunk * chunk_groups, (chunk + 1) * chunk_groups))
            return carry

        lax.fori_loop(1, n_chunks, more, 0)
        return carry

    lax.fori_loop(1, LOCAL, phase, 0)

    pltpu.make_async_copy(meta_recv, meta_recv, meta_recv_sem).wait()
    meta_in = meta_recv[:, 0, :].astype(jnp.bfloat16)
    of_source = onehot(iota((SOURCES, members), 0) == (iota((SOURCES, members), 1) >> 3))

    def scale_of(index):
        kind = index >> 5
        return jnp.where(
            kind == 0, 16384.0, jnp.where(kind == 1, 128.0, jnp.where(kind == 2, 1.0, -BIG))
        )

    across = f32_dot(meta_in, of_source, TN) * scale_of(iota((DEVICES, members), 0))
    down = f32_dot(of_source, meta_in, TN) * scale_of(iota((members, DEVICES), 1))
    filled_counts = []
    for local in range(LOCAL):
        pick = (iota((DEVICES, members), 0) & 31) == local * SLOTS + (iota((DEVICES, members), 1) & 7)
        key_rows[local] = BIG + jnp.sum(jnp.where(pick, across, 0.0), axis=0, keepdims=True)
        pick = (iota((members, DEVICES), 1) & 31) == local * SLOTS + (iota((members, DEVICES), 0) & 7)
        key_cols[local] = BIG + jnp.sum(jnp.where(pick, down, 0.0), axis=1, keepdims=True)

    lane = iota((members, DEVICES), 1)
    slot_of_member = iota((members, DEVICES), 0) & 7
    back = jnp.zeros((SOURCES, DEVICES), jnp.float32)
    for local in range(LOCAL):
        pltpu.make_async_copy(recv.at[local], recv.at[local], recv_sem.at[local]).wait()
        values = jnp.concatenate(
            [recv[local, h].astype(jnp.float32).reshape(members, width) for h in range(2)], axis=1
        )
        order_row = key_rows[local]
        order_col = key_cols[local]
        count = jnp.sum(jnp.where(order_row < BIG, 1.0, 0.0), axis=1, keepdims=True)
        squares = jnp.sum(values * values, axis=1, keepdims=True)
        lengths = jnp.sqrt(squares + epsilon)
        averages = jnp.sum(values, axis=0, keepdims=True) / count
        norm = jnp.sum(averages * averages, axis=1, keepdims=True)
        centroid = (averages / jnp.sqrt(norm + epsilon)).astype(jnp.bfloat16).astype(jnp.float32)
        for h in range(2):
            half = centroid[:, h * width : (h + 1) * width]
            cent_mine[h, local : local + 1] = half
            cent_mine[h, local + LOCAL : local + LOCAL + 1] = half
        products = jnp.sum(values * centroid, axis=1, keepdims=True)
        inverse = 1.0 / lengths
        sim = products * inverse
        unit = (values * inverse).astype(jnp.bfloat16)
        similar = f32_dot(unit, unit, NT)
        best = jnp.max(jnp.where(order_col < order_row, similar, -1.0), axis=0, keepdims=True)
        best_of_source = jnp.where(
            iota((SOURCES, members), 0) == (iota((SOURCES, members), 1) >> 3), best, 0.0
        )
        to_lane = onehot(lane == local * SLOTS + slot_of_member)
        sim_lanes = jnp.where(lane == (LOCAL + local) * SLOTS + slot_of_member, sim, 0.0)
        for piece in thirds(best_of_source):
            back = back + jnp.dot(piece, to_lane, preferred_element_type=jnp.float32)
        for piece in thirds(sim_lanes):
            back = back + jnp.dot(of_source, piece, preferred_element_type=jnp.float32)

    back_send[:, 0, :] = back
    swap = pltpu.make_async_remote_copy(
        cent_mine.at[1 - feat],
        cent_other,
        cent_send_sem,
        cent_recv_sem,
        device_id=(dp, 1 - feat),
        device_id_type=MESH,
    )

    def back_out(k, tdp, tfeat):
        pltpu.make_async_remote_copy(
            back_send.at[tdp],
            back_recv.at[dp * 2 + feat],
            back_send_sem,
            back_recv_sem,
            device_id=(tdp, tfeat),
            device_id_type=MESH,
        ).start()

    each_device(place, back_out)
    pltpu.make_async_copy(back_send.at[dp], back_recv.at[dp * 2 + feat], back_recv_sem).start()
    swap.start()

    pltpu.make_async_copy(back_recv, back_recv, back_recv_sem).wait()
    table = back_recv[:, 0, :]
    hits = hits_owner[...]
    found = jnp.zeros((DEVICES, n_rows), jnp.float32)
    for piece in thirds(table):
        found = found + f32_dot(piece, hits, TN)
    own_slot = slot_of_row[...] & 31
    line = iota((own_slots, n_rows), 0)
    mine = line == own_slot
    best_ref[...] = jnp.sum(jnp.where(mine, found[:own_slots], 0.0), axis=0, keepdims=True)
    sim_ref[...] = jnp.sum(
        jnp.where(mine, found[own_slots : 2 * own_slots], 0.0), axis=0, keepdims=True
    )
    swap.wait()
    owned_here = (iota((2 * LOCAL, width), 0) // LOCAL) == feat
    cent_ref[...] = jnp.where(owned_here, cent_mine[feat], cent_other[...]).astype(jnp.bfloat16)

    for local in range(LOCAL):
        sent = send.at[local, pl.ds(0, DEVICES - 1)]
        pltpu.make_async_copy(sent, sent, send_sem.at[local]).wait()
    sent = meta_send.at[pl.ds(0, SOURCES - 1)]
    pltpu.make_async_copy(sent, sent, meta_send_sem).wait()
    sent = back_recv.at[pl.ds(0, DEVICES - 1)]
    pltpu.make_async_copy(sent, sent, back_send_sem).wait()


def body(embeddings, assignments, order_index, cluster_blocks):
    n_rows, width = embeddings.shape
    members = SOURCES * SLOTS
    vmem = pl.BlockSpec(memory_space=pltpu.VMEM)
    dma = pltpu.SemaphoreType.DMA
    centroids, sims, bests = pl.pallas_call(
        kernel,
        out_shape=(
            jax.ShapeDtypeStruct((2 * LOCAL, width), jnp.bfloat16),
            jax.ShapeDtypeStruct((1, n_rows), jnp.float32),
            jax.ShapeDtypeStruct((1, n_rows), jnp.float32),
        ),
        in_specs=[pl.BlockSpec(memory_space=pl.ANY), vmem, vmem],
        out_specs=(vmem, vmem, vmem),
        scratch_shapes=[
            pltpu.VMEM((n_rows, width), jnp.bfloat16),
            pltpu.VMEM((1, n_rows), jnp.int32),
            pltpu.VMEM((DEVICES, n_rows), jnp.bfloat16),
            pltpu.VMEM((LOCAL, DEVICES, SLOTS, width), jnp.bfloat16),
            pltpu.VMEM((LOCAL, 2, SOURCES, SLOTS, width), jnp.bfloat16),
            pltpu.VMEM((DEVICES, 1, DEVICES), jnp.float32),
            pltpu.VMEM((SOURCES, 1, DEVICES), jnp.float32),
            pltpu.VMEM((LOCAL, members, 1), jnp.float32),
            pltpu.VMEM((LOCAL, 1, members), jnp.float32),
            pltpu.VMEM((2, 2 * LOCAL, width), jnp.float32),
            pltpu.VMEM((2 * LOCAL, width), jnp.float32),
            pltpu.VMEM((SOURCES, 1, DEVICES), jnp.float32),
            pltpu.VMEM((DEVICES, 1, DEVICES), jnp.float32),
            dma(()),
            dma((LOCAL,)),
            dma((LOCAL,)),
            dma(()),
            dma(()),
            dma(()),
            dma(()),
            dma(()),
            dma(()),
        ],
        compiler_params=pltpu.CompilerParams(
            collective_id=0, has_side_effects=True, vmem_limit_bytes=56 * 2**20
        ),
        name="dedup_window",
    )(embeddings, assignments.reshape(1, n_rows), order_index.reshape(1, n_rows))
    return centroids, sims.reshape(n_rows), bests.reshape(n_rows)


def solution(mesh):
    return jax.shard_map(
        body,
        mesh=mesh,
        in_specs=(P("dp", "feat"), P("dp"), P("dp"), P()),
        out_specs=(P("dp", "feat"), P("dp"), P("dp")),
        check_vma=False,
    )
```

```python
from functools import partial

import jax
import jax.numpy as jnp
from jax import lax
from jax.experimental import pallas as pl
from jax.experimental.pallas import tpu as pltpu
from jax.sharding import PartitionSpec as P

epsilon = 1e-06
MESH = pl.DeviceIdType.MESH
NT = (((1,), (1,)), ((), ()))
TN = (((0,), (0,)), ((), ()))

LOCAL = 4
SLOTS = 8
SOURCES = 64
DEVICES = 128
CHUNK = 32
BIG = float(2**20)


def iota(shape, axis):
    return lax.broadcasted_iota(jnp.int32, shape, axis)


def position():
    dp = lax.axis_index("dp")
    feat = lax.axis_index("feat")
    return dp, feat, (dp // 16, (dp // 4) % 4, (dp // 2) % 2 * 2 + feat, dp % 2)


def far_first(a):
    return (2 - a + a // 2 * 3 + a // 3 * 2) % 4


def each_device(place, visit, groups=(0, 8)):
    z, y, x, core = place
    planes = [(z + far_first(d)) % 4 * 16 for d in range(4)]
    lines = [(y + far_first(d)) % 4 * 4 for d in range(4)]
    corners = [planes[i % 4] + lines[i // 4] for i in range(16)]

    def column(group, carry):
        tx = (x + far_first(group % 4)) % 4
        tc = (core + 1 - group // 4) % 2
        inner = tx // 2 * 2 + tc
        for i in range(15 if isinstance(group, int) else 16):
            visit(group * 16 + i, corners[i] + inner, tx % 2)
        return carry

    first, last = groups
    if isinstance(last, int) and last == 8:
        if first < 7:
            lax.fori_loop(first, 7, column, 0)
        column(7, 0)
    else:
        lax.fori_loop(first, last, column, 0)


def owner_at(place, k):
    z, y, x, core = place

    def shift(a):
        return 2 - a + (a >> 1) * 3 + ((a + 1) >> 2) * 2

    tz = (z + shift(k & 3)) & 3
    ty = (y + shift((k >> 2) & 3)) & 3
    tx = (x + shift((k >> 4) & 3)) & 3
    tc = (core + 1 - (k >> 6)) & 1
    return (tz << 5) + (ty << 3) + ((tx >> 1) << 2) + (tc << 1) + (tx & 1)


def onehot(condition):
    return jnp.where(condition, 1.0, 0.0).astype(jnp.bfloat16)


def thirds(values):
    high = values.astype(jnp.bfloat16)
    rest = values - high.astype(jnp.float32)
    middle = rest.astype(jnp.bfloat16)
    low = (rest - middle.astype(jnp.float32)).astype(jnp.bfloat16)
    return high, middle, low


def f32_dot(a, b, dims):
    return lax.dot_general(a, b, dims, preferred_element_type=jnp.float32)


def kernel(
    rows_hbm,
    assign_hbm,
    order_hbm,
    cent_ref,
    sim_ref,
    best_ref,
    assign_ref,
    order_ref,
    rows,
    slot_of_row,
    hits_owner,
    send,
    recv,
    meta_send,
    meta_recv,
    key_cols,
    key_rows,
    cent_mine,
    cent_other,
    back_send,
    back_recv,
    load_sems,
    send_sem,
    recv_sem,
    meta_send_sem,
    meta_recv_sem,
    cent_send_sem,
    cent_recv_sem,
    back_send_sem,
    back_recv_sem,
):
    dp, feat, place = position()
    n_rows = rows.shape[0]
    width = rows.shape[1]
    members = SOURCES * SLOTS
    barrier = pltpu.get_barrier_semaphore()

    def greet(k, tdp, tfeat):
        pl.semaphore_signal(barrier, inc=1, device_id=(tdp, tfeat), device_id_type=MESH)

    each_device(place, greet)
    load_assign = pltpu.make_async_copy(assign_hbm, assign_ref, load_sems.at[0])
    load_order = pltpu.make_async_copy(order_hbm, order_ref, load_sems.at[1])
    load_rows = pltpu.make_async_copy(rows_hbm, rows, load_sems.at[2])
    load_assign.start()
    load_order.start()
    load_rows.start()

    part = 256
    n_clusters = DEVICES * LOCAL
    before = onehot(iota((part, part), 0) < iota((part, part), 1))
    ones = jnp.ones((part, part), jnp.bfloat16)

    load_assign.wait()
    counted = jnp.zeros((n_clusters, part), jnp.float32)
    for block in range(n_rows // part):
        piece = assign_ref[:, block * part : (block + 1) * part]
        member = iota((n_clusters, part), 0) == piece
        member_b = onehot(member)
        ahead = jnp.dot(member_b, before, preferred_element_type=jnp.float32) + counted
        rank = jnp.sum(jnp.where(member, ahead, 0.0), axis=0, keepdims=True)
        slot_of_row[:, block * part : (block + 1) * part] = piece * SLOTS + rank.astype(jnp.int32)
        if block + 1 < n_rows // part:
            counted = counted + jnp.dot(member_b, ones, preferred_element_type=jnp.float32)

    slots = slot_of_row[...]
    own_slots = LOCAL * SLOTS
    hits_owner[...] = onehot(iota((DEVICES, n_rows), 0) == (slots >> 5))
    load_order.wait()
    orders = order_ref[...]
    line = iota((DEVICES, n_rows), 0)
    kind = line >> 5
    digit = jnp.where(
        kind == 0,
        orders >> 14,
        jnp.where(kind == 1, (orders >> 7) & 127, jnp.where(kind == 2, orders & 127, 1)),
    )
    digits = jnp.where((line & 31) == (slots & 31), digit, 0).astype(jnp.float32)
    meta = f32_dot(hits_owner[...], digits.astype(jnp.bfloat16), NT)
    meta_send[:, 0, :] = meta

    def pack(local, chunk):
        q = iota((CHUNK * SLOTS, 1), 0)
        owner = owner_at(place, chunk * CHUNK + (q >> 3))
        wanted = owner * own_slots + local * SLOTS + (q & 7)
        hits = onehot(wanted == slot_of_row[...])
        packed = jnp.dot(hits, rows[...], preferred_element_type=jnp.float32)
        send[local, pl.ds(chunk * CHUNK, CHUNK)] = packed.reshape(CHUNK, SLOTS, width).astype(
            jnp.bfloat16
        )

    def ship_to(local):
        def ship(k, tdp, tfeat):
            pltpu.make_async_remote_copy(
                send.at[local, k],
                recv.at[local, feat, dp],
                send_sem.at[local],
                recv_sem.at[local],
                device_id=(tdp, tfeat),
                device_id_type=MESH,
            ).start()

        return ship

    def keep(local):
        pltpu.make_async_copy(
            send.at[local, DEVICES - 1], recv.at[local, feat, dp], recv_sem.at[local]
        ).start()

    n_chunks = DEVICES // CHUNK
    chunk_groups = CHUNK // 16

    def pack_first(chunk, carry):
        pack(0, chunk)
        return carry

    load_rows.wait()
    lax.fori_loop(0, n_chunks, pack_first, 0)
    pl.semaphore_wait(barrier, DEVICES - 1)
    each_device(place, ship_to(0))
    keep(0)

    z, y, x, core = place

    def meta_out(group, carry):
        tz = (z + group // 4) % 4
        ty = (y + group % 4) % 4
        for i in range(4):
            tdp = ((tz * 4 + ty) * 2 + (x // 2 + i // 2) % 2) * 2 + (core + i) % 2

            def start():
                pltpu.make_async_remote_copy(
                    meta_send.at[tdp * 2 + feat],
                    meta_recv.at[dp],
                    meta_send_sem,
                    meta_recv_sem,
                    device_id=(tdp, feat),
                    device_id_type=MESH,
                ).start()

            if i == 0:
                pl.when(group > 0)(start)
            else:
                start()
        return carry

    lax.fori_loop(0, 16, meta_out, 0)
    pltpu.make_async_copy(meta_send.at[dp * 2 + feat], meta_recv.at[dp], meta_recv_sem).start()

    def phase(local, carry):
        def ahead(chunk, carry):
            pack(local, chunk)
            each_device(place, ship_to(local), (chunk * chunk_groups, (chunk + 1) * chunk_groups))
            return carry

        lax.fori_loop(0, n_chunks - 1, ahead, 0)
        pack(local, n_chunks - 1)
        each_device(place, ship_to(local), (8 - chunk_groups, 8))
        keep(local)
        return carry

    lax.fori_loop(1, LOCAL, phase, 0)

    pltpu.make_async_copy(meta_recv, meta_recv, meta_recv_sem).wait()
    meta_in = meta_recv[:, 0, :].astype(jnp.bfloat16)
    of_source = onehot(iota((SOURCES, members), 0) == (iota((SOURCES, members), 1) >> 3))

    def scale_of(index):
        kind = index >> 5
        return jnp.where(
            kind == 0, 16384.0, jnp.where(kind == 1, 128.0, jnp.where(kind == 2, 1.0, -BIG))
        )

    across = f32_dot(meta_in, of_source, TN) * scale_of(iota((DEVICES, members), 0))
    down = f32_dot(of_source, meta_in, TN) * scale_of(iota((members, DEVICES), 1))
    filled_counts = []
    for local in range(LOCAL):
        pick = (iota((DEVICES, members), 0) & 31) == local * SLOTS + (iota((DEVICES, members), 1) & 7)
        key_rows[local] = BIG + jnp.sum(jnp.where(pick, across, 0.0), axis=0, keepdims=True)
        pick = (iota((members, DEVICES), 1) & 31) == local * SLOTS + (iota((members, DEVICES), 0) & 7)
        key_cols[local] = BIG + jnp.sum(jnp.where(pick, down, 0.0), axis=1, keepdims=True)

    lane = iota((members, DEVICES), 1)
    slot_of_member = iota((members, DEVICES), 0) & 7
    back = jnp.zeros((SOURCES, DEVICES), jnp.float32)
    for local in range(LOCAL):
        pltpu.make_async_copy(recv.at[local], recv.at[local], recv_sem.at[local]).wait()
        values = jnp.concatenate(
            [recv[local, h].astype(jnp.float32).reshape(members, width) for h in range(2)], axis=1
        )
        order_row = key_rows[local]
        order_col = key_cols[local]
        count = jnp.sum(jnp.where(order_row < BIG, 1.0, 0.0), axis=1, keepdims=True)
        squares = jnp.sum(values * values, axis=1, keepdims=True)
        lengths = jnp.sqrt(squares + epsilon)
        averages = jnp.sum(values, axis=0, keepdims=True) / count
        norm = jnp.sum(averages * averages, axis=1, keepdims=True)
        centroid = (averages / jnp.sqrt(norm + epsilon)).astype(jnp.bfloat16).astype(jnp.float32)
        for h in range(2):
            half = centroid[:, h * width : (h + 1) * width]
            cent_mine[h, local : local + 1] = half
            cent_mine[h, local + LOCAL : local + LOCAL + 1] = half
        products = jnp.sum(values * centroid, axis=1, keepdims=True)
        inverse = 1.0 / lengths
        sim = products * inverse
        unit = (values * inverse).astype(jnp.bfloat16)
        similar = f32_dot(unit, unit, NT)
        best = jnp.max(jnp.where(order_col < order_row, similar, -1.0), axis=0, keepdims=True)
        best_of_source = jnp.where(
            iota((SOURCES, members), 0) == (iota((SOURCES, members), 1) >> 3), best, 0.0
        )
        to_lane = onehot(lane == local * SLOTS + slot_of_member)
        sim_lanes = jnp.where(lane == (LOCAL + local) * SLOTS + slot_of_member, sim, 0.0)
        for piece in thirds(best_of_source):
            back = back + jnp.dot(piece, to_lane, preferred_element_type=jnp.float32)
        for piece in thirds(sim_lanes):
            back = back + jnp.dot(of_source, piece, preferred_element_type=jnp.float32)

    back_send[:, 0, :] = back
    swap = pltpu.make_async_remote_copy(
        cent_mine.at[1 - feat],
        cent_other,
        cent_send_sem,
        cent_recv_sem,
        device_id=(dp, 1 - feat),
        device_id_type=MESH,
    )

    def back_out(k, tdp, tfeat):
        pltpu.make_async_remote_copy(
            back_send.at[tdp],
            back_recv.at[dp * 2 + feat],
            back_send_sem,
            back_recv_sem,
            device_id=(tdp, tfeat),
            device_id_type=MESH,
        ).start()

    each_device(place, back_out)
    pltpu.make_async_copy(back_send.at[dp], back_recv.at[dp * 2 + feat], back_recv_sem).start()
    swap.start()

    pltpu.make_async_copy(back_recv, back_recv, back_recv_sem).wait()
    table = back_recv[:, 0, :]
    hits = hits_owner[...]
    found = jnp.zeros((DEVICES, n_rows), jnp.float32)
    for piece in thirds(table):
        found = found + f32_dot(piece, hits, TN)
    own_slot = slot_of_row[...] & 31
    line = iota((own_slots, n_rows), 0)
    mine = line == own_slot
    best_ref[...] = jnp.sum(jnp.where(mine, found[:own_slots], 0.0), axis=0, keepdims=True)
    sim_ref[...] = jnp.sum(
        jnp.where(mine, found[own_slots : 2 * own_slots], 0.0), axis=0, keepdims=True
    )
    swap.wait()
    owned_here = (iota((2 * LOCAL, width), 0) // LOCAL) == feat
    cent_ref[...] = jnp.where(owned_here, cent_mine[feat], cent_other[...]).astype(jnp.bfloat16)

    for local in range(LOCAL):
        sent = send.at[local, pl.ds(0, DEVICES - 1)]
        pltpu.make_async_copy(sent, sent, send_sem.at[local]).wait()
    sent = meta_send.at[pl.ds(0, SOURCES - 1)]
    pltpu.make_async_copy(sent, sent, meta_send_sem).wait()
    sent = back_recv.at[pl.ds(0, DEVICES - 1)]
    pltpu.make_async_copy(sent, sent, back_send_sem).wait()


def body(embeddings, assignments, order_index, cluster_blocks):
    n_rows, width = embeddings.shape
    members = SOURCES * SLOTS
    vmem = pl.BlockSpec(memory_space=pltpu.VMEM)
    dma = pltpu.SemaphoreType.DMA
    centroids, sims, bests = pl.pallas_call(
        kernel,
        out_shape=(
            jax.ShapeDtypeStruct((2 * LOCAL, width), jnp.bfloat16),
            jax.ShapeDtypeStruct((1, n_rows), jnp.float32),
            jax.ShapeDtypeStruct((1, n_rows), jnp.float32),
        ),
        in_specs=[pl.BlockSpec(memory_space=pl.ANY)] * 3,
        out_specs=(vmem, vmem, vmem),
        scratch_shapes=[
            pltpu.VMEM((1, n_rows), jnp.int32),
            pltpu.VMEM((1, n_rows), jnp.int32),
            pltpu.VMEM((n_rows, width), jnp.bfloat16),
            pltpu.VMEM((1, n_rows), jnp.int32),
            pltpu.VMEM((DEVICES, n_rows), jnp.bfloat16),
            pltpu.VMEM((LOCAL, DEVICES, SLOTS, width), jnp.bfloat16),
            pltpu.VMEM((LOCAL, 2, SOURCES, SLOTS, width), jnp.bfloat16),
            pltpu.VMEM((DEVICES, 1, DEVICES), jnp.float32),
            pltpu.VMEM((SOURCES, 1, DEVICES), jnp.float32),
            pltpu.VMEM((LOCAL, members, 1), jnp.float32),
            pltpu.VMEM((LOCAL, 1, members), jnp.float32),
            pltpu.VMEM((2, 2 * LOCAL, width), jnp.float32),
            pltpu.VMEM((2 * LOCAL, width), jnp.float32),
            pltpu.VMEM((SOURCES, 1, DEVICES), jnp.float32),
            pltpu.VMEM((DEVICES, 1, DEVICES), jnp.float32),
            dma((3,)),
            dma((LOCAL,)),
            dma((LOCAL,)),
            dma(()),
            dma(()),
            dma(()),
            dma(()),
            dma(()),
            dma(()),
        ],
        compiler_params=pltpu.CompilerParams(
            collective_id=0, has_side_effects=True, vmem_limit_bytes=56 * 2**20
        ),
        name="dedup_window",
    )(embeddings, assignments.reshape(1, n_rows), order_index.reshape(1, n_rows))
    return centroids, sims.reshape(n_rows), bests.reshape(n_rows)


def solution(mesh):
    return jax.shard_map(
        body,
        mesh=mesh,
        in_specs=(P("dp", "feat"), P("dp"), P("dp"), P()),
        out_specs=(P("dp", "feat"), P("dp"), P("dp")),
        check_vma=False,
    )
```

```python
from functools import partial

import jax
import jax.numpy as jnp
from jax import lax
from jax.experimental import pallas as pl
from jax.experimental.pallas import tpu as pltpu
from jax.sharding import PartitionSpec as P

epsilon = 1e-06
MESH = pl.DeviceIdType.MESH
NT = (((1,), (1,)), ((), ()))
TN = (((0,), (0,)), ((), ()))

LOCAL = 4
SLOTS = 8
SOURCES = 64
DEVICES = 128
CHUNK = 32
BIG = float(2**20)


def iota(shape, axis):
    return lax.broadcasted_iota(jnp.int32, shape, axis)


def position():
    dp = lax.axis_index("dp")
    feat = lax.axis_index("feat")
    return dp, feat, (dp // 16, (dp // 4) % 4, (dp // 2) % 2 * 2 + feat, dp % 2)


def far_first(a):
    return (2 - a + a // 2 * 3 + a // 3 * 2) % 4


def each_device(place, visit, groups=(0, 8)):
    z, y, x, core = place
    planes = [(z + far_first(d)) % 4 * 16 for d in range(4)]
    lines = [(y + far_first(d)) % 4 * 4 for d in range(4)]
    corners = [planes[i % 4] + lines[i // 4] for i in range(16)]

    def column(group, carry):
        tx = (x + far_first(group % 4)) % 4
        tc = (core + 1 - group // 4) % 2
        inner = tx // 2 * 2 + tc
        for i in range(15 if isinstance(group, int) else 16):
            visit(group * 16 + i, corners[i] + inner, tx % 2)
        return carry

    first, last = groups
    if isinstance(last, int) and last == 8:
        if first < 7:
            lax.fori_loop(first, 7, column, 0)
        column(7, 0)
    else:
        lax.fori_loop(first, last, column, 0)


def owner_at(place, k):
    z, y, x, core = place

    def shift(a):
        return 2 - a + (a >> 1) * 3 + ((a + 1) >> 2) * 2

    tz = (z + shift(k & 3)) & 3
    ty = (y + shift((k >> 2) & 3)) & 3
    tx = (x + shift((k >> 4) & 3)) & 3
    tc = (core + 1 - (k >> 6)) & 1
    return (tz << 5) + (ty << 3) + ((tx >> 1) << 2) + (tc << 1) + (tx & 1)


def onehot(condition):
    return jnp.where(condition, 1.0, 0.0).astype(jnp.bfloat16)


def thirds(values):
    high = values.astype(jnp.bfloat16)
    rest = values - high.astype(jnp.float32)
    middle = rest.astype(jnp.bfloat16)
    low = (rest - middle.astype(jnp.float32)).astype(jnp.bfloat16)
    return high, middle, low


def f32_dot(a, b, dims):
    return lax.dot_general(a, b, dims, preferred_element_type=jnp.float32)


def kernel(
    rows_hbm,
    assign_hbm,
    order_hbm,
    cent_ref,
    sim_ref,
    best_ref,
    assign_ref,
    order_ref,
    rows,
    slot_of_row,
    hits_owner,
    send,
    recv,
    meta_send,
    meta_recv,
    key_cols,
    key_rows,
    cent_mine,
    cent_other,
    back_send,
    back_recv,
    load_sems,
    send_sem,
    recv_sem,
    meta_send_sem,
    meta_recv_sem,
    cent_send_sem,
    cent_recv_sem,
    back_send_sem,
    back_recv_sem,
):
    dp, feat, place = position()
    n_rows = rows.shape[0]
    width = rows.shape[1]
    members = SOURCES * SLOTS
    barrier = pltpu.get_barrier_semaphore()

    def greet(k, tdp, tfeat):
        pl.semaphore_signal(barrier, inc=1, device_id=(tdp, tfeat), device_id_type=MESH)

    each_device(place, greet)
    load_assign = pltpu.make_async_copy(assign_hbm, assign_ref, load_sems.at[0])
    load_order = pltpu.make_async_copy(order_hbm, order_ref, load_sems.at[1])
    load_rows = pltpu.make_async_copy(rows_hbm, rows, load_sems.at[2])
    load_assign.start()
    load_order.start()
    load_rows.start()

    part = 256
    n_clusters = DEVICES * LOCAL
    before = onehot(iota((part, part), 0) < iota((part, part), 1))
    ones = jnp.ones((part, part), jnp.bfloat16)

    load_assign.wait()
    counted = jnp.zeros((n_clusters, part), jnp.float32)
    for block in range(n_rows // part):
        piece = assign_ref[:, block * part : (block + 1) * part]
        member = iota((n_clusters, part), 0) == piece
        member_b = onehot(member)
        ahead = jnp.dot(member_b, before, preferred_element_type=jnp.float32) + counted
        rank = jnp.sum(jnp.where(member, ahead, 0.0), axis=0, keepdims=True)
        slot_of_row[:, block * part : (block + 1) * part] = piece * SLOTS + rank.astype(jnp.int32)
        if block + 1 < n_rows // part:
            counted = counted + jnp.dot(member_b, ones, preferred_element_type=jnp.float32)

    own_slots = LOCAL * SLOTS

    def pack(local, chunk):
        q = iota((CHUNK * SLOTS, 1), 0)
        owner = owner_at(place, chunk * CHUNK + (q >> 3))
        wanted = owner * own_slots + local * SLOTS + (q & 7)
        hits = onehot(wanted == slot_of_row[...])
        packed = jnp.dot(hits, rows[...], preferred_element_type=jnp.float32)
        send[local, pl.ds(chunk * CHUNK, CHUNK)] = packed.reshape(CHUNK, SLOTS, width).astype(
            jnp.bfloat16
        )

    def ship_to(local):
        def ship(k, tdp, tfeat):
            pltpu.make_async_remote_copy(
                send.at[local, k],
                recv.at[local, feat, dp],
                send_sem.at[local],
                recv_sem.at[local],
                device_id=(tdp, tfeat),
                device_id_type=MESH,
            ).start()

        return ship

    def keep(local):
        pltpu.make_async_copy(
            send.at[local, DEVICES - 1], recv.at[local, feat, dp], recv_sem.at[local]
        ).start()

    n_chunks = DEVICES // CHUNK
    chunk_groups = CHUNK // 16

    def ahead_of(local):
        def ahead(chunk, carry):
            pack(local, chunk)
            each_device(place, ship_to(local), (chunk * chunk_groups, (chunk + 1) * chunk_groups))
            return carry

        return ahead

    def finish(local):
        pack(local, n_chunks - 1)
        each_device(place, ship_to(local), (8 - chunk_groups, 8))
        keep(local)

    load_rows.wait()
    pack(0, 0)
    pl.semaphore_wait(barrier, DEVICES - 1)
    each_device(place, ship_to(0), (0, chunk_groups))
    lax.fori_loop(1, n_chunks - 1, ahead_of(0), 0)
    finish(0)

    slots = slot_of_row[...]
    hits_owner[...] = onehot(iota((DEVICES, n_rows), 0) == (slots >> 5))
    load_order.wait()
    orders = order_ref[...]
    line = iota((DEVICES, n_rows), 0)
    kind = line >> 5
    digit = jnp.where(
        kind == 0,
        orders >> 14,
        jnp.where(kind == 1, (orders >> 7) & 127, jnp.where(kind == 2, orders & 127, 1)),
    )
    digits = jnp.where((line & 31) == (slots & 31), digit, 0).astype(jnp.float32)
    meta = f32_dot(hits_owner[...], digits.astype(jnp.bfloat16), NT)
    meta_send[:, 0, :] = meta

    z, y, x, core = place

    def meta_out(group, carry):
        tz = (z + group // 4) % 4
        ty = (y + group % 4) % 4
        for i in range(4):
            tdp = ((tz * 4 + ty) * 2 + (x // 2 + i // 2) % 2) * 2 + (core + i) % 2

            def start():
                pltpu.make_async_remote_copy(
                    meta_send.at[tdp * 2 + feat],
                    meta_recv.at[dp],
                    meta_send_sem,
                    meta_recv_sem,
                    device_id=(tdp, feat),
                    device_id_type=MESH,
                ).start()

            if i == 0:
                pl.when(group > 0)(start)
            else:
                start()
        return carry

    lax.fori_loop(0, 16, meta_out, 0)
    pltpu.make_async_copy(meta_send.at[dp * 2 + feat], meta_recv.at[dp], meta_recv_sem).start()

    def phase(local, carry):
        lax.fori_loop(0, n_chunks - 1, ahead_of(local), 0)
        finish(local)
        return carry

    lax.fori_loop(1, LOCAL, phase, 0)

    pltpu.make_async_copy(meta_recv, meta_recv, meta_recv_sem).wait()
    meta_in = meta_recv[:, 0, :].astype(jnp.bfloat16)
    of_source = onehot(iota((SOURCES, members), 0) == (iota((SOURCES, members), 1) >> 3))

    def scale_of(index):
        kind = index >> 5
        return jnp.where(
            kind == 0, 16384.0, jnp.where(kind == 1, 128.0, jnp.where(kind == 2, 1.0, -BIG))
        )

    across = f32_dot(meta_in, of_source, TN) * scale_of(iota((DEVICES, members), 0))
    down = f32_dot(of_source, meta_in, TN) * scale_of(iota((members, DEVICES), 1))
    filled_counts = []
    for local in range(LOCAL):
        pick = (iota((DEVICES, members), 0) & 31) == local * SLOTS + (iota((DEVICES, members), 1) & 7)
        key_rows[local] = BIG + jnp.sum(jnp.where(pick, across, 0.0), axis=0, keepdims=True)
        pick = (iota((members, DEVICES), 1) & 31) == local * SLOTS + (iota((members, DEVICES), 0) & 7)
        key_cols[local] = BIG + jnp.sum(jnp.where(pick, down, 0.0), axis=1, keepdims=True)

    lane = iota((members, DEVICES), 1)
    slot_of_member = iota((members, DEVICES), 0) & 7
    back = jnp.zeros((SOURCES, DEVICES), jnp.float32)
    for local in range(LOCAL):
        pltpu.make_async_copy(recv.at[local], recv.at[local], recv_sem.at[local]).wait()
        values = jnp.concatenate(
            [recv[local, h].astype(jnp.float32).reshape(members, width) for h in range(2)], axis=1
        )
        order_row = key_rows[local]
        order_col = key_cols[local]
        count = jnp.sum(jnp.where(order_row < BIG, 1.0, 0.0), axis=1, keepdims=True)
        squares = jnp.sum(values * values, axis=1, keepdims=True)
        lengths = jnp.sqrt(squares + epsilon)
        averages = jnp.sum(values, axis=0, keepdims=True) / count
        norm = jnp.sum(averages * averages, axis=1, keepdims=True)
        centroid = (averages / jnp.sqrt(norm + epsilon)).astype(jnp.bfloat16).astype(jnp.float32)
        for h in range(2):
            half = centroid[:, h * width : (h + 1) * width]
            cent_mine[h, local : local + 1] = half
            cent_mine[h, local + LOCAL : local + LOCAL + 1] = half
        products = jnp.sum(values * centroid, axis=1, keepdims=True)
        inverse = 1.0 / lengths
        sim = products * inverse
        unit = (values * inverse).astype(jnp.bfloat16)
        similar = f32_dot(unit, unit, NT)
        best = jnp.max(jnp.where(order_col < order_row, similar, -1.0), axis=0, keepdims=True)
        best_of_source = jnp.where(
            iota((SOURCES, members), 0) == (iota((SOURCES, members), 1) >> 3), best, 0.0
        )
        to_lane = onehot(lane == local * SLOTS + slot_of_member)
        sim_lanes = jnp.where(lane == (LOCAL + local) * SLOTS + slot_of_member, sim, 0.0)
        for piece in thirds(best_of_source):
            back = back + jnp.dot(piece, to_lane, preferred_element_type=jnp.float32)
        for piece in thirds(sim_lanes):
            back = back + jnp.dot(of_source, piece, preferred_element_type=jnp.float32)

    back_send[:, 0, :] = back
    swap = pltpu.make_async_remote_copy(
        cent_mine.at[1 - feat],
        cent_other,
        cent_send_sem,
        cent_recv_sem,
        device_id=(dp, 1 - feat),
        device_id_type=MESH,
    )

    def back_out(k, tdp, tfeat):
        pltpu.make_async_remote_copy(
            back_send.at[tdp],
            back_recv.at[dp * 2 + feat],
            back_send_sem,
            back_recv_sem,
            device_id=(tdp, tfeat),
            device_id_type=MESH,
        ).start()

    each_device(place, back_out)
    pltpu.make_async_copy(back_send.at[dp], back_recv.at[dp * 2 + feat], back_recv_sem).start()
    swap.start()

    pltpu.make_async_copy(back_recv, back_recv, back_recv_sem).wait()
    table = back_recv[:, 0, :]
    hits = hits_owner[...]
    found = jnp.zeros((DEVICES, n_rows), jnp.float32)
    for piece in thirds(table):
        found = found + f32_dot(piece, hits, TN)
    own_slot = slot_of_row[...] & 31
    line = iota((own_slots, n_rows), 0)
    mine = line == own_slot
    best_ref[...] = jnp.sum(jnp.where(mine, found[:own_slots], 0.0), axis=0, keepdims=True)
    sim_ref[...] = jnp.sum(
        jnp.where(mine, found[own_slots : 2 * own_slots], 0.0), axis=0, keepdims=True
    )
    swap.wait()
    owned_here = (iota((2 * LOCAL, width), 0) // LOCAL) == feat
    cent_ref[...] = jnp.where(owned_here, cent_mine[feat], cent_other[...]).astype(jnp.bfloat16)

    for local in range(LOCAL):
        sent = send.at[local, pl.ds(0, DEVICES - 1)]
        pltpu.make_async_copy(sent, sent, send_sem.at[local]).wait()
    sent = meta_send.at[pl.ds(0, SOURCES - 1)]
    pltpu.make_async_copy(sent, sent, meta_send_sem).wait()
    sent = back_recv.at[pl.ds(0, DEVICES - 1)]
    pltpu.make_async_copy(sent, sent, back_send_sem).wait()


def hand_over(*refs):
    for source, target in zip(refs[:3], refs[3:]):
        target[...] = source[...]


def body(embeddings, assignments, order_index, cluster_blocks):
    n_rows, width = embeddings.shape
    members = SOURCES * SLOTS
    vmem = pl.BlockSpec(memory_space=pltpu.VMEM)
    dma = pltpu.SemaphoreType.DMA
    centroids, sims, bests = pl.pallas_call(
        kernel,
        out_shape=(
            jax.ShapeDtypeStruct((2 * LOCAL, width), jnp.bfloat16),
            jax.ShapeDtypeStruct((1, n_rows), jnp.float32),
            jax.ShapeDtypeStruct((1, n_rows), jnp.float32),
        ),
        in_specs=[pl.BlockSpec(memory_space=pl.ANY)] * 3,
        out_specs=(vmem, vmem, vmem),
        scratch_shapes=[
            pltpu.VMEM((1, n_rows), jnp.int32),
            pltpu.VMEM((1, n_rows), jnp.int32),
            pltpu.VMEM((n_rows, width), jnp.bfloat16),
            pltpu.VMEM((1, n_rows), jnp.int32),
            pltpu.VMEM((DEVICES, n_rows), jnp.bfloat16),
            pltpu.VMEM((LOCAL, DEVICES, SLOTS, width), jnp.bfloat16),
            pltpu.VMEM((LOCAL, 2, SOURCES, SLOTS, width), jnp.bfloat16),
            pltpu.VMEM((DEVICES, 1, DEVICES), jnp.float32),
            pltpu.VMEM((SOURCES, 1, DEVICES), jnp.float32),
            pltpu.VMEM((LOCAL, members, 1), jnp.float32),
            pltpu.VMEM((LOCAL, 1, members), jnp.float32),
            pltpu.VMEM((2, 2 * LOCAL, width), jnp.float32),
            pltpu.VMEM((2 * LOCAL, width), jnp.float32),
            pltpu.VMEM((SOURCES, 1, DEVICES), jnp.float32),
            pltpu.VMEM((DEVICES, 1, DEVICES), jnp.float32),
            dma((3,)),
            dma((LOCAL,)),
            dma((LOCAL,)),
            dma(()),
            dma(()),
            dma(()),
            dma(()),
            dma(()),
            dma(()),
        ],
        compiler_params=pltpu.CompilerParams(
            collective_id=0, has_side_effects=True, vmem_limit_bytes=56 * 2**20
        ),
        name="dedup_window",
    )(embeddings, assignments.reshape(1, n_rows), order_index.reshape(1, n_rows))
    outs = tuple(jax.ShapeDtypeStruct(x.shape, x.dtype) for x in (centroids, sims, bests))
    centroids, sims, bests = pl.pallas_call(
        hand_over, out_shape=outs, in_specs=[vmem] * 3, out_specs=(vmem,) * 3, name="hand_over"
    )(centroids, sims, bests)
    return centroids, sims.reshape(n_rows), bests.reshape(n_rows)


def solution(mesh):
    return jax.shard_map(
        body,
        mesh=mesh,
        in_specs=(P("dp", "feat"), P("dp"), P("dp"), P()),
        out_specs=(P("dp", "feat"), P("dp"), P("dp")),
        check_vma=False,
    )
```

```python
from functools import partial

import jax
import jax.numpy as jnp
from jax import lax
from jax.experimental import pallas as pl
from jax.experimental.pallas import tpu as pltpu
from jax.sharding import PartitionSpec as P

epsilon = 1e-06
MESH = pl.DeviceIdType.MESH
NT = (((1,), (1,)), ((), ()))
TN = (((0,), (0,)), ((), ()))

LOCAL = 4
SLOTS = 8
SOURCES = 64
DEVICES = 128
CHUNK = 32
BIG = float(2**20)


def iota(shape, axis):
    return lax.broadcasted_iota(jnp.int32, shape, axis)


def position():
    dp = lax.axis_index("dp")
    feat = lax.axis_index("feat")
    return dp, feat, (dp // 16, (dp // 4) % 4, (dp // 2) % 2 * 2 + feat, dp % 2)


def far_first(a):
    return (2 - a + a // 2 * 3 + a // 3 * 2) % 4


def each_device(place, visit, groups=(0, 8), unrolled=False):
    z, y, x, core = place
    planes = [(z + far_first(d)) % 4 * 16 for d in range(4)]
    lines = [(y + far_first(d)) % 4 * 4 for d in range(4)]
    corners = [planes[i % 4] + lines[i // 4] for i in range(16)]

    def column(group, carry):
        tx = (x + far_first(group % 4)) % 4
        tc = (core + 1 - group // 4) % 2
        inner = tx // 2 * 2 + tc
        for i in range(15 if isinstance(group, int) and group == 7 else 16):
            visit(group * 16 + i, corners[i] + inner, tx % 2)
        return carry

    if unrolled:
        for group in range(*groups):
            column(group, 0)
        return
    first, last = groups
    if isinstance(last, int) and last == 8:
        if first < 7:
            lax.fori_loop(first, 7, column, 0)
        column(7, 0)
    else:
        lax.fori_loop(first, last, column, 0)


def owner_at(place, k):
    z, y, x, core = place

    def shift(a):
        return 2 - a + (a >> 1) * 3 + ((a + 1) >> 2) * 2

    tz = (z + shift(k & 3)) & 3
    ty = (y + shift((k >> 2) & 3)) & 3
    tx = (x + shift((k >> 4) & 3)) & 3
    tc = (core + 1 - (k >> 6)) & 1
    return (tz << 5) + (ty << 3) + ((tx >> 1) << 2) + (tc << 1) + (tx & 1)


def onehot(condition):
    return jnp.where(condition, 1.0, 0.0).astype(jnp.bfloat16)


def thirds(values):
    high = values.astype(jnp.bfloat16)
    rest = values - high.astype(jnp.float32)
    middle = rest.astype(jnp.bfloat16)
    low = (rest - middle.astype(jnp.float32)).astype(jnp.bfloat16)
    return high, middle, low


def f32_dot(a, b, dims):
    return lax.dot_general(a, b, dims, preferred_element_type=jnp.float32)


def kernel(
    rows_hbm,
    assign_hbm,
    order_hbm,
    cent_ref,
    sim_ref,
    best_ref,
    assign_ref,
    order_ref,
    rows,
    slot_of_row,
    hits_owner,
    send,
    recv,
    meta_send,
    meta_recv,
    key_cols,
    key_rows,
    cent_mine,
    cent_other,
    back_send,
    back_recv,
    load_sems,
    send_sem,
    recv_sem,
    meta_send_sem,
    meta_recv_sem,
    cent_send_sem,
    cent_recv_sem,
    back_send_sem,
    back_recv_sem,
):
    dp, feat, place = position()
    n_rows = rows.shape[0]
    width = rows.shape[1]
    members = SOURCES * SLOTS
    barrier = pltpu.get_barrier_semaphore()

    def greet(k, tdp, tfeat):
        pl.semaphore_signal(barrier, inc=1, device_id=(tdp, tfeat), device_id_type=MESH)

    each_device(place, greet, unrolled=True)
    load_assign = pltpu.make_async_copy(assign_hbm, assign_ref, load_sems.at[0])
    load_order = pltpu.make_async_copy(order_hbm, order_ref, load_sems.at[1])
    load_rows = pltpu.make_async_copy(rows_hbm, rows, load_sems.at[2])
    load_assign.start()
    load_order.start()
    load_rows.start()

    part = 256
    n_clusters = DEVICES * LOCAL
    before = onehot(iota((part, part), 0) < iota((part, part), 1))
    ones = jnp.ones((part, part), jnp.bfloat16)

    load_assign.wait()
    counted = jnp.zeros((n_clusters, part), jnp.float32)
    for block in range(n_rows // part):
        piece = assign_ref[:, block * part : (block + 1) * part]
        member = iota((n_clusters, part), 0) == piece
        member_b = onehot(member)
        ahead = jnp.dot(member_b, before, preferred_element_type=jnp.float32) + counted
        rank = jnp.sum(jnp.where(member, ahead, 0.0), axis=0, keepdims=True)
        slot_of_row[:, block * part : (block + 1) * part] = piece * SLOTS + rank.astype(jnp.int32)
        if block + 1 < n_rows // part:
            counted = counted + jnp.dot(member_b, ones, preferred_element_type=jnp.float32)

    own_slots = LOCAL * SLOTS

    def pack(local, chunk):
        q = iota((CHUNK * SLOTS, 1), 0)
        owner = owner_at(place, chunk * CHUNK + (q >> 3))
        wanted = owner * own_slots + local * SLOTS + (q & 7)
        hits = onehot(wanted == slot_of_row[...])
        packed = jnp.dot(hits, rows[...], preferred_element_type=jnp.float32)
        send[local, pl.ds(chunk * CHUNK, CHUNK)] = packed.reshape(CHUNK, SLOTS, width).astype(
            jnp.bfloat16
        )

    def ship_to(local):
        def ship(k, tdp, tfeat):
            pltpu.make_async_remote_copy(
                send.at[local, k],
                recv.at[local, feat, dp],
                send_sem.at[local],
                recv_sem.at[local],
                device_id=(tdp, tfeat),
                device_id_type=MESH,
            ).start()

        return ship

    def keep(local):
        pltpu.make_async_copy(
            send.at[local, DEVICES - 1], recv.at[local, feat, dp], recv_sem.at[local]
        ).start()

    n_chunks = DEVICES // CHUNK
    chunk_groups = CHUNK // 16

    def ahead_of(local):
        def ahead(chunk, carry):
            pack(local, chunk)
            each_device(place, ship_to(local), (chunk * chunk_groups, (chunk + 1) * chunk_groups))
            return carry

        return ahead

    def finish(local):
        pack(local, n_chunks - 1)
        each_device(place, ship_to(local), (8 - chunk_groups, 8))
        keep(local)

    load_rows.wait()
    pack(0, 0)
    pl.semaphore_wait(barrier, DEVICES - 1)
    each_device(place, ship_to(0), (0, chunk_groups))
    lax.fori_loop(1, n_chunks - 1, ahead_of(0), 0)
    finish(0)

    slots = slot_of_row[...]
    hits_owner[...] = onehot(iota((DEVICES, n_rows), 0) == (slots >> 5))
    load_order.wait()
    orders = order_ref[...]
    line = iota((DEVICES, n_rows), 0)
    kind = line >> 5
    digit = jnp.where(
        kind == 0,
        orders >> 14,
        jnp.where(kind == 1, (orders >> 7) & 127, jnp.where(kind == 2, orders & 127, 1)),
    )
    digits = jnp.where((line & 31) == (slots & 31), digit, 0).astype(jnp.float32)
    meta = f32_dot(hits_owner[...], digits.astype(jnp.bfloat16), NT)
    meta_send[:, 0, :] = meta

    z, y, x, core = place

    def meta_out(group, carry):
        tz = (z + group // 4) % 4
        ty = (y + group % 4) % 4
        for i in range(4):
            tdp = ((tz * 4 + ty) * 2 + (x // 2 + i // 2) % 2) * 2 + (core + i) % 2

            def start():
                pltpu.make_async_remote_copy(
                    meta_send.at[tdp * 2 + feat],
                    meta_recv.at[dp],
                    meta_send_sem,
                    meta_recv_sem,
                    device_id=(tdp, feat),
                    device_id_type=MESH,
                ).start()

            if i == 0:
                pl.when(group > 0)(start)
            else:
                start()
        return carry

    lax.fori_loop(0, 16, meta_out, 0)
    pltpu.make_async_copy(meta_send.at[dp * 2 + feat], meta_recv.at[dp], meta_recv_sem).start()

    def phase(local, carry):
        lax.fori_loop(0, n_chunks - 1, ahead_of(local), 0)
        finish(local)
        return carry

    lax.fori_loop(1, LOCAL, phase, 0)

    pltpu.make_async_copy(meta_recv, meta_recv, meta_recv_sem).wait()
    meta_in = meta_recv[:, 0, :].astype(jnp.bfloat16)
    of_source = onehot(iota((SOURCES, members), 0) == (iota((SOURCES, members), 1) >> 3))

    def scale_of(index):
        kind = index >> 5
        return jnp.where(
            kind == 0, 16384.0, jnp.where(kind == 1, 128.0, jnp.where(kind == 2, 1.0, -BIG))
        )

    across = f32_dot(meta_in, of_source, TN) * scale_of(iota((DEVICES, members), 0))
    down = f32_dot(of_source, meta_in, TN) * scale_of(iota((members, DEVICES), 1))
    filled_counts = []
    for local in range(LOCAL):
        pick = (iota((DEVICES, members), 0) & 31) == local * SLOTS + (iota((DEVICES, members), 1) & 7)
        key_rows[local] = BIG + jnp.sum(jnp.where(pick, across, 0.0), axis=0, keepdims=True)
        pick = (iota((members, DEVICES), 1) & 31) == local * SLOTS + (iota((members, DEVICES), 0) & 7)
        key_cols[local] = BIG + jnp.sum(jnp.where(pick, down, 0.0), axis=1, keepdims=True)

    lane = iota((members, DEVICES), 1)
    slot_of_member = iota((members, DEVICES), 0) & 7
    def own(local, back):
        pltpu.make_async_copy(recv.at[local], recv.at[local], recv_sem.at[local]).wait()
        values = jnp.concatenate(
            [recv[local, h].astype(jnp.float32).reshape(members, width) for h in range(2)], axis=1
        )
        order_row = key_rows[local]
        order_col = key_cols[local]
        count = jnp.sum(jnp.where(order_row < BIG, 1.0, 0.0), axis=1, keepdims=True)
        squares = jnp.sum(values * values, axis=1, keepdims=True)
        lengths = jnp.sqrt(squares + epsilon)
        averages = jnp.sum(values, axis=0, keepdims=True) / count
        norm = jnp.sum(averages * averages, axis=1, keepdims=True)
        centroid = (averages / jnp.sqrt(norm + epsilon)).astype(jnp.bfloat16).astype(jnp.float32)
        for h in range(2):
            cent_mine[h, local] = centroid[:, h * width : (h + 1) * width]
        products = jnp.sum(values * centroid, axis=1, keepdims=True)
        inverse = 1.0 / lengths
        sim = products * inverse
        unit = (values * inverse).astype(jnp.bfloat16)
        similar = f32_dot(unit, unit, NT)
        best = jnp.max(jnp.where(order_col < order_row, similar, -1.0), axis=0, keepdims=True)
        best_of_source = jnp.where(
            iota((SOURCES, members), 0) == (iota((SOURCES, members), 1) >> 3), best, 0.0
        )
        to_lane = onehot(lane == local * SLOTS + slot_of_member)
        sim_lanes = jnp.where(lane == (LOCAL + local) * SLOTS + slot_of_member, sim, 0.0)
        for piece in thirds(best_of_source):
            back = back + jnp.dot(piece, to_lane, preferred_element_type=jnp.float32)
        for piece in thirds(sim_lanes):
            back = back + jnp.dot(of_source, piece, preferred_element_type=jnp.float32)
        return back

    back = lax.fori_loop(0, LOCAL, own, jnp.zeros((SOURCES, DEVICES), jnp.float32))
    back_send[:, 0, :] = back
    swap = pltpu.make_async_remote_copy(
        cent_mine.at[1 - feat],
        cent_other,
        cent_send_sem,
        cent_recv_sem,
        device_id=(dp, 1 - feat),
        device_id_type=MESH,
    )

    def back_out(k, tdp, tfeat):
        pltpu.make_async_remote_copy(
            back_send.at[tdp],
            back_recv.at[dp * 2 + feat],
            back_send_sem,
            back_recv_sem,
            device_id=(tdp, tfeat),
            device_id_type=MESH,
        ).start()

    each_device(place, back_out, unrolled=True)
    pltpu.make_async_copy(back_send.at[dp], back_recv.at[dp * 2 + feat], back_recv_sem).start()
    swap.start()

    pltpu.make_async_copy(back_recv, back_recv, back_recv_sem).wait()
    table = back_recv[:, 0, :][:, : 2 * own_slots]
    hits = hits_owner[...]
    found = jnp.zeros((2 * own_slots, n_rows), jnp.float32)
    for piece in thirds(table):
        found = found + f32_dot(piece, hits, TN)
    own_slot = slot_of_row[...] & 31
    line = iota((own_slots, n_rows), 0)
    mine = line == own_slot
    best_ref[...] = jnp.sum(jnp.where(mine, found[:own_slots], 0.0), axis=0, keepdims=True)
    sim_ref[...] = jnp.sum(
        jnp.where(mine, found[own_slots : 2 * own_slots], 0.0), axis=0, keepdims=True
    )
    swap.wait()
    mine = [cent_mine[feat, local] for local in range(LOCAL)]
    other = [cent_other[local] for local in range(LOCAL)]
    owned_here = (iota((2 * LOCAL, width), 0) // LOCAL) == feat
    cent_ref[...] = jnp.where(
        owned_here, jnp.concatenate(mine + mine), jnp.concatenate(other + other)
    ).astype(jnp.bfloat16)

    for local in range(LOCAL):
        sent = send.at[local, pl.ds(0, DEVICES - 1)]
        pltpu.make_async_copy(sent, sent, send_sem.at[local]).wait()
    sent = meta_send.at[pl.ds(0, SOURCES - 1)]
    pltpu.make_async_copy(sent, sent, meta_send_sem).wait()
    sent = back_recv.at[pl.ds(0, DEVICES - 1)]
    pltpu.make_async_copy(sent, sent, back_send_sem).wait()


def hand_over(*refs):
    for source, target in zip(refs[:3], refs[3:]):
        target[...] = source[...]


def body(embeddings, assignments, order_index, cluster_blocks):
    n_rows, width = embeddings.shape
    members = SOURCES * SLOTS
    vmem = pl.BlockSpec(memory_space=pltpu.VMEM)
    dma = pltpu.SemaphoreType.DMA
    centroids, sims, bests = pl.pallas_call(
        kernel,
        out_shape=(
            jax.ShapeDtypeStruct((2 * LOCAL, width), jnp.bfloat16),
            jax.ShapeDtypeStruct((1, n_rows), jnp.float32),
            jax.ShapeDtypeStruct((1, n_rows), jnp.float32),
        ),
        in_specs=[pl.BlockSpec(memory_space=pl.ANY)] * 3,
        out_specs=(vmem, vmem, vmem),
        scratch_shapes=[
            pltpu.VMEM((1, n_rows), jnp.int32),
            pltpu.VMEM((1, n_rows), jnp.int32),
            pltpu.VMEM((n_rows, width), jnp.bfloat16),
            pltpu.VMEM((1, n_rows), jnp.int32),
            pltpu.VMEM((DEVICES, n_rows), jnp.bfloat16),
            pltpu.VMEM((LOCAL, DEVICES, SLOTS, width), jnp.bfloat16),
            pltpu.VMEM((LOCAL, 2, SOURCES, SLOTS, width), jnp.bfloat16),
            pltpu.VMEM((DEVICES, 1, DEVICES), jnp.float32),
            pltpu.VMEM((SOURCES, 1, DEVICES), jnp.float32),
            pltpu.VMEM((LOCAL, members, 1), jnp.float32),
            pltpu.VMEM((LOCAL, 1, members), jnp.float32),
            pltpu.VMEM((2, LOCAL, 1, width), jnp.float32),
            pltpu.VMEM((LOCAL, 1, width), jnp.float32),
            pltpu.VMEM((SOURCES, 1, DEVICES), jnp.float32),
            pltpu.VMEM((DEVICES, 1, DEVICES), jnp.float32),
            dma((3,)),
            dma((LOCAL,)),
            dma((LOCAL,)),
            dma(()),
            dma(()),
            dma(()),
            dma(()),
            dma(()),
            dma(()),
        ],
        compiler_params=pltpu.CompilerParams(
            collective_id=0, has_side_effects=True, vmem_limit_bytes=32 * 2**20
        ),
        name="dedup_window",
    )(*[pltpu.with_memory_space_constraint(x, pltpu.HBM) for x in (embeddings, assignments.reshape(1, n_rows), order_index.reshape(1, n_rows))])
    outs = tuple(jax.ShapeDtypeStruct(x.shape, x.dtype) for x in (centroids, sims, bests))
    centroids, sims, bests = pl.pallas_call(
        hand_over, out_shape=outs, in_specs=[vmem] * 3, out_specs=(vmem,) * 3, compiler_params=pltpu.CompilerParams(vmem_limit_bytes=2**20), name="hand_over"
    )(centroids, sims, bests)
    return centroids, sims.reshape(n_rows), bests.reshape(n_rows)


def solution(mesh):
    return jax.shard_map(
        body,
        mesh=mesh,
        in_specs=(P("dp", "feat"), P("dp"), P("dp"), P()),
        out_specs=(P("dp", "feat"), P("dp"), P("dp")),
        check_vma=False,
    )
```

```python
from functools import partial

import jax
import jax.numpy as jnp
from jax import lax
from jax.experimental import pallas as pl
from jax.experimental.pallas import tpu as pltpu
from jax.sharding import PartitionSpec as P

epsilon = 1e-06
MESH = pl.DeviceIdType.MESH
NT = (((1,), (1,)), ((), ()))
TN = (((0,), (0,)), ((), ()))

LOCAL = 4
SLOTS = 8
SOURCES = 64
DEVICES = 128
CHUNK = 32
BIG = float(2**20)


def iota(shape, axis):
    return lax.broadcasted_iota(jnp.int32, shape, axis)


def position():
    dp = lax.axis_index("dp")
    feat = lax.axis_index("feat")
    return dp, feat, (dp // 16, (dp // 4) % 4, (dp // 2) % 2 * 2 + feat, dp % 2)


def far_first(a):
    return (2 - a + a // 2 * 3 + a // 3 * 2) % 4


def each_device(place, visit, groups=(0, 8), unrolled=False):
    z, y, x, core = place
    planes = [(z + far_first(d)) % 4 * 16 for d in range(4)]
    lines = [(y + far_first(d)) % 4 * 4 for d in range(4)]
    corners = [planes[i % 4] + lines[i // 4] for i in range(16)]

    def column(group, carry):
        tx = (x + far_first(group % 4)) % 4
        tc = (core + 1 - group // 4) % 2
        inner = tx // 2 * 2 + tc
        for i in range(15 if isinstance(group, int) and group == 7 else 16):
            visit(group * 16 + i, corners[i] + inner, tx % 2)
        return carry

    if unrolled:
        for group in range(*groups):
            column(group, 0)
        return
    first, last = groups
    if isinstance(last, int) and last == 8:
        if first < 7:
            lax.fori_loop(first, 7, column, 0)
        column(7, 0)
    else:
        lax.fori_loop(first, last, column, 0)


def owner_at(place, k):
    z, y, x, core = place

    def shift(a):
        return 2 - a + (a >> 1) * 3 + ((a + 1) >> 2) * 2

    tz = (z + shift(k & 3)) & 3
    ty = (y + shift((k >> 2) & 3)) & 3
    tx = (x + shift((k >> 4) & 3)) & 3
    tc = (core + 1 - (k >> 6)) & 1
    return (tz << 5) + (ty << 3) + ((tx >> 1) << 2) + (tc << 1) + (tx & 1)


def onehot(condition):
    return jnp.where(condition, 1.0, 0.0).astype(jnp.bfloat16)


def thirds(values):
    high = values.astype(jnp.bfloat16)
    rest = values - high.astype(jnp.float32)
    middle = rest.astype(jnp.bfloat16)
    low = (rest - middle.astype(jnp.float32)).astype(jnp.bfloat16)
    return high, middle, low


def f32_dot(a, b, dims):
    return lax.dot_general(a, b, dims, preferred_element_type=jnp.float32)


def kernel(
    rows_hbm,
    assign_hbm,
    order_hbm,
    cent_ref,
    sim_ref,
    best_ref,
    assign_ref,
    order_ref,
    rows,
    slot_of_row,
    hits_owner,
    send,
    recv,
    meta_send,
    meta_recv,
    key_cols,
    key_rows,
    cent_mine,
    cent_other,
    back_send,
    back_recv,
    load_sems,
    send_sem,
    recv_sem,
    meta_send_sem,
    meta_recv_sem,
    cent_send_sem,
    cent_recv_sem,
    back_send_sem,
    back_recv_sem,
):
    dp, feat, place = position()
    n_rows = rows.shape[0]
    width = rows.shape[1]
    members = SOURCES * SLOTS
    barrier = pltpu.get_barrier_semaphore()

    def greet(k, tdp, tfeat):
        pl.semaphore_signal(barrier, inc=1, device_id=(tdp, tfeat), device_id_type=MESH)

    each_device(place, greet, unrolled=True)
    load_assign = pltpu.make_async_copy(assign_hbm, assign_ref, load_sems.at[0])
    load_order = pltpu.make_async_copy(order_hbm, order_ref, load_sems.at[1])
    load_rows = pltpu.make_async_copy(rows_hbm, rows, load_sems.at[2])
    load_assign.start()
    load_order.start()
    load_rows.start()

    part = 256
    n_clusters = DEVICES * LOCAL
    before = onehot(iota((part, part), 0) < iota((part, part), 1))
    ones = jnp.ones((part, part), jnp.bfloat16)

    load_assign.wait()
    counted = jnp.zeros((n_clusters, part), jnp.float32)
    for block in range(n_rows // part):
        piece = assign_ref[:, block * part : (block + 1) * part]
        member = iota((n_clusters, part), 0) == piece
        member_b = onehot(member)
        ahead = jnp.dot(member_b, before, preferred_element_type=jnp.float32) + counted
        rank = jnp.sum(jnp.where(member, ahead, 0.0), axis=0, keepdims=True)
        slot_of_row[:, block * part : (block + 1) * part] = piece * SLOTS + rank.astype(jnp.int32)
        if block + 1 < n_rows // part:
            counted = counted + jnp.dot(member_b, ones, preferred_element_type=jnp.float32)

    own_slots = LOCAL * SLOTS

    def pack(local, chunk):
        q = iota((CHUNK * SLOTS, 1), 0)
        owner = owner_at(place, chunk * CHUNK + (q >> 3))
        wanted = owner * own_slots + local * SLOTS + (q & 7)
        hits = onehot(wanted == slot_of_row[...])
        packed = jnp.dot(hits, rows[...], preferred_element_type=jnp.float32)
        send[local, pl.ds(chunk * CHUNK, CHUNK)] = packed.reshape(CHUNK, SLOTS, width).astype(
            jnp.bfloat16
        )

    def ship_to(local):
        def ship(k, tdp, tfeat):
            pltpu.make_async_remote_copy(
                send.at[local, k],
                recv.at[local, feat, dp],
                send_sem.at[local],
                recv_sem.at[local],
                device_id=(tdp, tfeat),
                device_id_type=MESH,
            ).start()

        return ship

    def keep(local):
        pltpu.make_async_copy(
            send.at[local, DEVICES - 1], recv.at[local, feat, dp], recv_sem.at[local]
        ).start()

    n_chunks = DEVICES // CHUNK
    chunk_groups = CHUNK // 16

    def ahead_of(local):
        def ahead(chunk, carry):
            pack(local, chunk)
            each_device(place, ship_to(local), (chunk * chunk_groups, (chunk + 1) * chunk_groups))
            return carry

        return ahead

    def finish(local):
        pack(local, n_chunks - 1)
        each_device(place, ship_to(local), (8 - chunk_groups, 8))
        keep(local)

    load_rows.wait()
    pack(0, 0)
    pl.semaphore_wait(barrier, DEVICES - 1)
    each_device(place, ship_to(0), (0, chunk_groups))
    lax.fori_loop(1, n_chunks - 1, ahead_of(0), 0)
    finish(0)

    slots = slot_of_row[...]
    hits_owner[...] = onehot(iota((DEVICES, n_rows), 0) == (slots >> 5))
    load_order.wait()
    orders = order_ref[...]
    line = iota((DEVICES, n_rows), 0)
    kind = line >> 5
    digit = jnp.where(
        kind == 0,
        orders >> 14,
        jnp.where(kind == 1, (orders >> 7) & 127, jnp.where(kind == 2, orders & 127, 1)),
    )
    digits = jnp.where((line & 31) == (slots & 31), digit, 0).astype(jnp.float32)
    meta = f32_dot(hits_owner[...], digits.astype(jnp.bfloat16), NT)
    meta_send[:, 0, :] = meta

    z, y, x, core = place

    def meta_out(group, carry):
        tz = (z + group // 4) % 4
        ty = (y + group % 4) % 4
        for i in range(4):
            tdp = ((tz * 4 + ty) * 2 + (x // 2 + i // 2) % 2) * 2 + (core + i) % 2

            def start():
                pltpu.make_async_remote_copy(
                    meta_send.at[tdp * 2 + feat],
                    meta_recv.at[dp],
                    meta_send_sem,
                    meta_recv_sem,
                    device_id=(tdp, feat),
                    device_id_type=MESH,
                ).start()

            if i == 0:
                pl.when(group > 0)(start)
            else:
                start()
        return carry

    lax.fori_loop(0, 16, meta_out, 0)
    pltpu.make_async_copy(meta_send.at[dp * 2 + feat], meta_recv.at[dp], meta_recv_sem).start()

    def phase(local, carry):
        lax.fori_loop(0, n_chunks - 1, ahead_of(local), 0)
        finish(local)
        return carry

    lax.fori_loop(1, LOCAL, phase, 0)

    pltpu.make_async_copy(meta_recv, meta_recv, meta_recv_sem).wait()
    meta_in = meta_recv[:, 0, :].astype(jnp.bfloat16)
    of_source = onehot(iota((SOURCES, members), 0) == (iota((SOURCES, members), 1) >> 3))

    def scale_of(index):
        kind = index >> 5
        return jnp.where(
            kind == 0, 16384.0, jnp.where(kind == 1, 128.0, jnp.where(kind == 2, 1.0, -BIG))
        )

    across = f32_dot(meta_in, of_source, TN) * scale_of(iota((DEVICES, members), 0))
    down = f32_dot(of_source, meta_in, TN) * scale_of(iota((members, DEVICES), 1))
    filled_counts = []
    for local in range(LOCAL):
        pick = (iota((DEVICES, members), 0) & 31) == local * SLOTS + (iota((DEVICES, members), 1) & 7)
        key_rows[local] = BIG + jnp.sum(jnp.where(pick, across, 0.0), axis=0, keepdims=True)
        pick = (iota((members, DEVICES), 1) & 31) == local * SLOTS + (iota((members, DEVICES), 0) & 7)
        key_cols[local] = BIG + jnp.sum(jnp.where(pick, down, 0.0), axis=1, keepdims=True)

    lane = iota((members, DEVICES), 1)
    slot_of_member = iota((members, DEVICES), 0) & 7
    def own(local, back):
        pltpu.make_async_copy(recv.at[local], recv.at[local], recv_sem.at[local]).wait()
        values = jnp.concatenate(
            [recv[local, h].astype(jnp.float32).reshape(members, width) for h in range(2)], axis=1
        )
        order_row = key_rows[local]
        order_col = key_cols[local]
        count = jnp.sum(jnp.where(order_row < BIG, 1.0, 0.0), axis=1, keepdims=True)
        squares = jnp.sum(values * values, axis=1, keepdims=True)
        lengths = jnp.sqrt(squares + epsilon)
        averages = jnp.sum(values, axis=0, keepdims=True) / count
        norm = jnp.sum(averages * averages, axis=1, keepdims=True)
        centroid = (averages / jnp.sqrt(norm + epsilon)).astype(jnp.bfloat16).astype(jnp.float32)
        for h in range(2):
            cent_mine[h, local] = centroid[:, h * width : (h + 1) * width]
        products = jnp.sum(values * centroid, axis=1, keepdims=True)
        inverse = 1.0 / lengths
        sim = products * inverse
        unit = (values * inverse).astype(jnp.bfloat16)
        similar = f32_dot(unit, unit, NT)
        best = jnp.max(jnp.where(order_col < order_row, similar, -1.0), axis=0, keepdims=True)
        best_of_source = jnp.where(
            iota((SOURCES, members), 0) == (iota((SOURCES, members), 1) >> 3), best, 0.0
        )
        to_lane = onehot(lane == local * SLOTS + slot_of_member)
        sim_lanes = jnp.where(lane == (LOCAL + local) * SLOTS + slot_of_member, sim, 0.0)
        left = jnp.concatenate([*thirds(best_of_source), of_source, of_source, of_source], axis=1)
        right = jnp.concatenate([to_lane, to_lane, to_lane, *thirds(sim_lanes)])
        back = back + jnp.dot(left, right, preferred_element_type=jnp.float32)
        return back

    back = lax.fori_loop(0, LOCAL, own, jnp.zeros((SOURCES, DEVICES), jnp.float32))
    back_send[:, 0, :] = back
    swap = pltpu.make_async_remote_copy(
        cent_mine.at[1 - feat],
        cent_other,
        cent_send_sem,
        cent_recv_sem,
        device_id=(dp, 1 - feat),
        device_id_type=MESH,
    )

    def back_out(k, tdp, tfeat):
        pltpu.make_async_remote_copy(
            back_send.at[tdp],
            back_recv.at[dp * 2 + feat],
            back_send_sem,
            back_recv_sem,
            device_id=(tdp, tfeat),
            device_id_type=MESH,
        ).start()

    each_device(place, back_out, unrolled=True)
    pltpu.make_async_copy(back_send.at[dp], back_recv.at[dp * 2 + feat], back_recv_sem).start()
    swap.start()

    swap.wait()
    mine = [cent_mine[feat, local] for local in range(LOCAL)]
    other = [cent_other[local] for local in range(LOCAL)]
    owned_here = (iota((2 * LOCAL, width), 0) // LOCAL) == feat
    cent_ref[...] = jnp.where(
        owned_here, jnp.concatenate(mine + mine), jnp.concatenate(other + other)
    ).astype(jnp.bfloat16)

    for local in range(LOCAL):
        sent = send.at[local, pl.ds(0, DEVICES - 1)]
        pltpu.make_async_copy(sent, sent, send_sem.at[local]).wait()
    sent = meta_send.at[pl.ds(0, SOURCES - 1)]
    pltpu.make_async_copy(sent, sent, meta_send_sem).wait()
    pltpu.make_async_copy(back_recv, back_recv, back_recv_sem).wait()
    table = back_recv[:, 0, :][:, : 2 * own_slots]
    hits = hits_owner[...]
    found = jnp.zeros((2 * own_slots, n_rows), jnp.float32)
    for piece in thirds(table):
        found = found + f32_dot(piece, hits, TN)
    own_slot = slot_of_row[...] & 31
    line = iota((own_slots, n_rows), 0)
    mine = line == own_slot
    best_ref[...] = jnp.sum(jnp.where(mine, found[:own_slots], 0.0), axis=0, keepdims=True)
    sim_ref[...] = jnp.sum(
        jnp.where(mine, found[own_slots : 2 * own_slots], 0.0), axis=0, keepdims=True
    )

    sent = back_recv.at[pl.ds(0, DEVICES - 1)]
    pltpu.make_async_copy(sent, sent, back_send_sem).wait()


def hand_over(*refs):
    for source, target in zip(refs[:3], refs[3:]):
        target[...] = source[...]


def body(embeddings, assignments, order_index, cluster_blocks):
    n_rows, width = embeddings.shape
    members = SOURCES * SLOTS
    vmem = pl.BlockSpec(memory_space=pltpu.VMEM)
    dma = pltpu.SemaphoreType.DMA
    centroids, sims, bests = pl.pallas_call(
        kernel,
        out_shape=(
            jax.ShapeDtypeStruct((2 * LOCAL, width), jnp.bfloat16),
            jax.ShapeDtypeStruct((1, n_rows), jnp.float32),
            jax.ShapeDtypeStruct((1, n_rows), jnp.float32),
        ),
        in_specs=[pl.BlockSpec(memory_space=pl.ANY)] * 3,
        out_specs=(vmem, vmem, vmem),
        scratch_shapes=[
            pltpu.VMEM((1, n_rows), jnp.int32),
            pltpu.VMEM((1, n_rows), jnp.int32),
            pltpu.VMEM((n_rows, width), jnp.bfloat16),
            pltpu.VMEM((1, n_rows), jnp.int32),
            pltpu.VMEM((DEVICES, n_rows), jnp.bfloat16),
            pltpu.VMEM((LOCAL, DEVICES, SLOTS, width), jnp.bfloat16),
            pltpu.VMEM((LOCAL, 2, SOURCES, SLOTS, width), jnp.bfloat16),
            pltpu.VMEM((DEVICES, 1, DEVICES), jnp.float32),
            pltpu.VMEM((SOURCES, 1, DEVICES), jnp.float32),
            pltpu.VMEM((LOCAL, members, 1), jnp.float32),
            pltpu.VMEM((LOCAL, 1, members), jnp.float32),
            pltpu.VMEM((2, LOCAL, 1, width), jnp.float32),
            pltpu.VMEM((LOCAL, 1, width), jnp.float32),
            pltpu.VMEM((SOURCES, 1, DEVICES), jnp.float32),
            pltpu.VMEM((DEVICES, 1, DEVICES), jnp.float32),
            dma((3,)),
            dma((LOCAL,)),
            dma((LOCAL,)),
            dma(()),
            dma(()),
            dma(()),
            dma(()),
            dma(()),
            dma(()),
        ],
        compiler_params=pltpu.CompilerParams(
            collective_id=0, has_side_effects=True, vmem_limit_bytes=32 * 2**20
        ),
        name="dedup_window",
    )(*[pltpu.with_memory_space_constraint(x, pltpu.HBM) for x in (embeddings, assignments.reshape(1, n_rows), order_index.reshape(1, n_rows))])
    outs = tuple(jax.ShapeDtypeStruct(x.shape, x.dtype) for x in (centroids, sims, bests))
    centroids, sims, bests = pl.pallas_call(
        hand_over, out_shape=outs, in_specs=[vmem] * 3, out_specs=(vmem,) * 3, compiler_params=pltpu.CompilerParams(vmem_limit_bytes=2**20), name="hand_over"
    )(centroids, sims, bests)
    return centroids, sims.reshape(n_rows), bests.reshape(n_rows)


def solution(mesh):
    return jax.shard_map(
        body,
        mesh=mesh,
        in_specs=(P("dp", "feat"), P("dp"), P("dp"), P()),
        out_specs=(P("dp", "feat"), P("dp"), P("dp")),
        check_vma=False,
    )
```
